32 devices in a mesh: mem: 4 (over x, core), lon: 8 (over z, y).
Axes of the slice: x: 2, y: 2, z: 4, core: 2. Of those that a mesh axis runs over, the one named last changes fastest.
Arguments:
- prior_fields: bfloat16 [80, 1536, 256], P('mem', 'lon'), may hold values from -6 to 6
- scaled_sensor_spread: bfloat16 [80, 1536, 256], P('mem', 'lon'), may hold values from -3 to 3
- measured_misfit: float32 [1536, 256], P('lon'), may hold values from -12 to 12
- inverse_error_variance: float32 [1536, 256], P('lon'), may hold values from 0.5 to 4
- active_sensor_number: int32 [1536], P('lon'), may hold values from 64 to 256, as said below
- adjacent_tiles: int32 [1536, 16], P('lon'), may hold values from 0 to 1535, as said below
Outputs:
- analysis: bfloat16 [80, 1536, 256], P('mem', 'lon')
The draws below stay inside these ranges and needn't reach their ends.
Inputs may be any that keep to these rules, and one draw needn't show every extreme that they name: `adjacent_tiles`: row b holds 16 different block indices, all within 48 blocks of b around the closed sequence of 1536 blocks; among them b itself and the blocks exactly 48 before and after b. Slots at and beyond active_sensor_number[c] of block c are padding; some block is full in every draw.
All inputs are finite; a program needn't handle non-finite values.
Results may differ from the reference program's by a relative error of at most 0.0069.
Values may be sent and summed in bfloat16 or wider, within the bound.
No kernel may reach another device: no remote copies, remote signals or barrier semaphores. Data moves between devices by JAX's collectives and lax.ppermute only.
A program may use at most 128 MiB of HBM per device.

```python
import math
import jax
import jax.numpy as jnp
from jax import lax

SAMPLE_NUMBER = 80
TILE_VALUE_TOTAL = 256
OBS_SLOTS = 256
RADIUS = 48
NEIGHBOURS = 16
SWEEPS = 5
BLK_LON = 192
BELT_TILES = 1536
N_LON = 8


def draw_active_sensor_number(key, part):
    first_key, second_key = jax.random.split(key)
    counts = jax.random.randint(first_key, (BELT_TILES,), OBS_SLOTS // 4, OBS_SLOTS + 1)
    full_block = jax.random.randint(second_key, (), 0, BELT_TILES)
    block_ids = jnp.arange(BELT_TILES, dtype=jnp.int32)
    return jnp.where(block_ids == full_block, OBS_SLOTS, counts).astype(jnp.int32)


def draw_adjacent_tiles(key, part):
    width_inner = 2 * RADIUS - 2
    inner = jnp.concatenate([jnp.arange(-(RADIUS - 1), 0, dtype=jnp.int32), jnp.arange(1, RADIUS, dtype=jnp.int32)])
    scores = jax.random.randint(key, (BELT_TILES, width_inner), 0, 1 << 20) * width_inner + jnp.arange(width_inner, dtype=jnp.int32)[None, :]
    ordering = jnp.argsort(scores, axis=1)
    picked = inner[ordering[:, :NEIGHBOURS - 3]]
    fixed_offsets = jnp.broadcast_to(jnp.array([0, -RADIUS, RADIUS], dtype=jnp.int32)[None, :], (BELT_TILES, 3))
    offsets = jnp.concatenate([fixed_offsets, picked], axis=1)
    block_ids = jnp.arange(BELT_TILES, dtype=jnp.int32)[:, None]
    return jnp.mod(block_ids + offsets, BELT_TILES).astype(jnp.int32)


def block_levels(rng, extent, shards, least, largest):
    loudness = 1.0
    for dim, shards_of in shards:
        draws = jax.random.uniform(jax.random.fold_in(jax.random.fold_in(rng, 6), dim), (shards_of,), jnp.float32, least / len(shards), largest / len(shards))
        loudness = loudness * jnp.repeat(jnp.exp(draws), extent[dim] // shards_of).reshape((-1,) + (1,) * (len(extent) - 1 - dim))
    return loudness


def gaussian(stream_key, extent, spread, most, pieces=(), held_as=jnp.bfloat16):
    entries = jax.random.normal(stream_key, extent, jnp.float32) * spread
    if len(pieces) > 0:
        entries = block_levels(stream_key, extent, pieces, -0.22, 0.18) * entries
    return jnp.clip(entries, min=-most, max=most).astype(held_as)


def setup_inputs(seed: int = 0) -> dict:
    key_of = jax.random.split(jax.random.key(seed), 7)
    prior_fields = gaussian(key_of[0], (SAMPLE_NUMBER, BELT_TILES, TILE_VALUE_TOTAL), 1.0, 6.0, ((0, 4), (1, 8)))
    scaled_sensor_spread = gaussian(key_of[1], (SAMPLE_NUMBER, BELT_TILES, OBS_SLOTS), 0.5, 3.0, ((0, 4), (1, 8)))
    measured_misfit = gaussian(key_of[2], (BELT_TILES, OBS_SLOTS), 2.0, 12.0, ((0, 8),), jnp.float32)
    inverse_error_variance = jnp.clip(jnp.exp(math.log(4.0) - 2.0794415 * jax.random.uniform(key_of[3], (BELT_TILES, OBS_SLOTS), jnp.float32) ** block_levels(key_of[3], (BELT_TILES, OBS_SLOTS), ((0, 8),), -0.2, 0.2)), 0.5, 4.0)
    active_sensor_number = draw_active_sensor_number(jax.random.fold_in(key_of[6], 71), 0)
    adjacent_tiles = draw_adjacent_tiles(jax.random.fold_in(key_of[6], 71), 0)
    return dict(prior_fields=prior_fields, scaled_sensor_spread=scaled_sensor_spread, measured_misfit=measured_misfit, inverse_error_variance=inverse_error_variance, active_sensor_number=active_sensor_number, adjacent_tiles=adjacent_tiles)


def taper_of(offset):
    ratio = offset.astype(jnp.float32) / RADIUS
    return 1.0 / (1.0 + ratio * ratio)

def inverse_root(matrix):
    identity = jnp.eye(matrix.shape[-1], dtype=jnp.float32)
    frobenius = jnp.sqrt(lax.optimization_barrier(jnp.sum(matrix * matrix, axis=(-2, -1))))
    iterate = matrix / frobenius[..., None, None]
    inv_root = jnp.broadcast_to(identity, matrix.shape)
    for sweep_index in range(SWEEPS):
        newton_step = 1.5 * identity - 0.5 * jnp.matmul(inv_root, iterate, precision=lax.Precision.HIGHEST)
        iterate = jnp.matmul(iterate, newton_step, precision=lax.Precision.HIGHEST)
        inv_root = jnp.matmul(newton_step, inv_root, precision=lax.Precision.HIGHEST)
    return inv_root / jnp.sqrt(frobenius)[..., None, None]

def reference(prior_fields, scaled_sensor_spread, measured_misfit, inverse_error_variance, active_sensor_number, adjacent_tiles):
    slot_ids = jnp.arange(OBS_SLOTS, dtype=jnp.int32)
    live_mask = (slot_ids[None, :] < active_sensor_number[:, None]).astype(jnp.float32)
    obs_scale = jnp.sqrt(inverse_error_variance * live_mask)
    scaled = (scaled_sensor_spread.astype(jnp.float32) * obs_scale[None]).astype(jnp.bfloat16).astype(jnp.float32)
    weighted = (measured_misfit * obs_scale).astype(jnp.bfloat16).astype(jnp.float32)
    grams = jnp.einsum('kto,jto->tkj', scaled, scaled, precision=lax.Precision.HIGHEST)
    pulls = jnp.einsum('kto,to->tk', scaled, weighted, precision=lax.Precision.HIGHEST)
    sample_fields = jnp.transpose(prior_fields, (1, 0, 2))
    identity = jnp.eye(SAMPLE_NUMBER, dtype=jnp.float32)

    def one_group(group_index):
        start_row = (group_index * BLK_LON).astype(jnp.int32)
        band_rows = lax.dynamic_slice_in_dim(adjacent_tiles, start_row, BLK_LON, 0)
        block_ids = start_row + jnp.arange(BLK_LON, dtype=jnp.int32)
        offset_raw = jnp.mod(band_rows - block_ids[:, None], BELT_TILES)
        offset = jnp.where(offset_raw > BELT_TILES // 2, offset_raw - BELT_TILES, offset_raw)
        tapers = taper_of(offset)
        picked = grams[band_rows]
        summed = lax.optimization_barrier(jnp.sum(tapers[:, :, None, None] * picked, axis=1))
        pulled = lax.optimization_barrier(jnp.sum(tapers[:, :, None] * pulls[band_rows], axis=1))
        matrix = identity + summed / (SAMPLE_NUMBER - 1)
        inv_root = inverse_root(matrix)
        inner = jnp.matmul(inv_root, pulled[..., None], precision=lax.Precision.HIGHEST)
        mean_shift = jnp.matmul(inv_root, inner, precision=lax.Precision.HIGHEST)[..., 0] / (SAMPLE_NUMBER - 1)
        blend = (inv_root + mean_shift[..., None]).astype(jnp.bfloat16).astype(jnp.float32)
        block_state = lax.dynamic_slice_in_dim(sample_fields, start_row, BLK_LON, 0).astype(jnp.float32)
        center = lax.optimization_barrier(jnp.mean(block_state, axis=1))
        anomalies = (block_state - center[:, None]).astype(jnp.bfloat16).astype(jnp.float32)
        mixed = jnp.einsum('bjs,bjk->bks', anomalies, blend, precision=lax.Precision.HIGHEST)
        return (center[:, None] + mixed).astype(jnp.bfloat16)
    result = lax.map(one_group, jnp.arange(N_LON, dtype=jnp.int32))
    result = result.reshape(BELT_TILES, SAMPLE_NUMBER, TILE_VALUE_TOTAL)
    return jnp.transpose(result, (1, 0, 2))
```

```python
import functools

import jax
import jax.numpy as jnp
from jax import lax
from jax.experimental import pallas as pl
from jax.experimental.pallas import tpu as pltpu
from jax.sharding import PartitionSpec as P

RADIUS = 48
SWEEPS = 5
LANES = 128
F32 = jnp.float32
BF16 = jnp.bfloat16
VMEM_BYTES = 56 * 1024 * 1024


def vmem():
    return pl.BlockSpec(memory_space=pltpu.VMEM)


def smem():
    return pl.BlockSpec(memory_space=pltpu.SMEM)


def params():
    return pltpu.CompilerParams(vmem_limit_bytes=VMEM_BYTES)


def gram_kernel(mem_ref, *refs, groups, share, blocks, width, unroll):
    parts = refs[:groups]
    scale_ref, weight_ref, own_ref, send_ref, rows_ref = refs[groups:]
    members = groups * share
    half = members // 2
    tiles = width // LANES
    mem = mem_ref[0]
    scale = scale_ref[...]
    for d in range(groups):
        base = (mem ^ d) * (share * blocks)

        def scale_member(k, carry, part=parts[d], base=base):
            value = (part[k].astype(F32) * scale).astype(BF16).astype(F32)
            start = pl.multiple_of(base + k * blocks, 8)
            for t in range(tiles):
                rows_ref[t, pl.ds(start, blocks), :] = value[:, t * LANES : (t + 1) * LANES]
            return carry

        lax.fori_loop(0, share, scale_member, 0, unroll=4)

    lane = lax.broadcasted_iota(jnp.int32, (half, LANES), 1)
    pull_lane = members + half
    from_top = (lane < members) | (lane == pull_lane) | (lane == pull_lane + 2)
    spare = LANES - pull_lane

    def block_group(i, carry):
        for u in range(unroll):
            b = i * unroll + u
            spread = jnp.concatenate(
                [rows_ref[t, pl.ds(b, members, stride=blocks), :] for t in range(tiles)], axis=1
            )
            weights = jnp.broadcast_to(weight_ref[pl.ds(b, 1), :], (spare, width))
            right = jnp.concatenate([spread, spread[half:], weights], axis=0).astype(BF16)
            product = lax.dot_general(
                spread.astype(BF16), right, (((1,), (1,)), ((), ())), preferred_element_type=F32
            )
            packed = jnp.where(from_top, product[:half], product[half:])
            own_ref[pl.ds(pl.multiple_of(b * half, 8), half), :] = packed
        return carry

    lax.fori_loop(0, blocks // unroll, block_group, 0)

    step = 2 * half
    lane2 = lax.broadcasted_iota(jnp.int32, (step, LANES), 1)

    def finish(i, carry):
        at = pl.ds(pl.multiple_of(i * step, 16), step)
        value = own_ref[at, :]
        low = value - value.astype(BF16).astype(F32)
        is_low = lane2 >= pull_lane + 2
        send_ref[at, :] = jnp.where(is_low, low, value).astype(BF16)
        own_ref[at, :] = jnp.where(is_low, 0.0, value)
        return carry

    lax.fori_loop(0, blocks // 2, finish, 0, unroll=2)


def packed_grams(mem, parts, scale, weighted):
    groups = len(parts)
    share, blocks, width = parts[0].shape
    members = groups * share
    half = members // 2
    assert members + half + 4 <= LANES and half % 8 == 0
    flat = (blocks * half, LANES)
    return pl.pallas_call(
        functools.partial(
            gram_kernel, groups=groups, share=share, blocks=blocks, width=width, unroll=4
        ),
        out_shape=(jax.ShapeDtypeStruct(flat, F32), jax.ShapeDtypeStruct(flat, BF16)),
        in_specs=[smem()] + [vmem()] * (groups + 2),
        out_specs=(vmem(), vmem()),
        scratch_shapes=[pltpu.VMEM((width // LANES, members * blocks, LANES), F32)],
        compiler_params=params(),
        cost_estimate=pl.CostEstimate(
            flops=2 * blocks * members * width * LANES,
            bytes_accessed=members * blocks * width * 2,
            transcendentals=0,
        ),
        name="packed_grams",
    )(mem, *parts, scale, weighted)


def blend_kernel(
    row_ref, taper_ref, left_ref, own_ref, right_ref, blend_ref, window_ref, *, members, neighbours, blocks, unroll
):
    half = members // 2
    pull_lane = members + half
    halo = left_ref.shape[0]
    count = own_ref.shape[0]
    window_ref[pl.ds(0, halo), :] = left_ref[...].astype(F32)
    window_ref[pl.ds(halo, count), :] = own_ref[...]
    window_ref[pl.ds(halo + count, halo), :] = right_ref[...].astype(F32)
    full = (members, LANES)
    lane = lax.broadcasted_iota(jnp.int32, full, 1)
    row = lax.broadcasted_iota(jnp.int32, full, 0)
    valid = lane < members
    eye = (lane == row).astype(F32)
    left_half = lax.broadcasted_iota(jnp.int32, (half, LANES), 1) < half
    pad_rows = jnp.zeros((LANES - half, LANES), F32)
    pad_depth = jnp.zeros((LANES - members, LANES), BF16)

    def total(x):
        return jnp.sum(jnp.sum(x, axis=0, keepdims=True), axis=1, keepdims=True)

    def times(lhs, rhs):
        return jnp.dot(
            lhs, jnp.concatenate([rhs, pad_depth], axis=0), preferred_element_type=F32
        )

    def one_block(b):
        packed = None
        for n in range(neighbours):
            start = pl.multiple_of(row_ref[b * neighbours + n], 8)
            term = taper_ref[b * neighbours + n] * window_ref[pl.ds(start, half), :]
            packed = term if packed is None else packed + term
        turned = jnp.concatenate([packed, pad_rows], axis=0).T
        low_rows = jnp.where(
            left_half, turned[half:members], pltpu.roll(packed, LANES - half, axis=1)
        )
        summed = jnp.concatenate([packed, low_rows], axis=0)
        matrix = eye + jnp.where(valid, summed, 0.0) * (1.0 / (members - 1))
        pull = turned[pull_lane : pull_lane + 8]
        pull_row = (pull[0:1] + pull[2:3]) + pltpu.roll(pull[1:2] + pull[3:4], half, axis=1)

        frob = jnp.sqrt(total(matrix * matrix))
        scaled = matrix * (1.0 / frob)
        y = total(scaled * eye) * (1.0 / members)
        y_rest = scaled - y * eye
        p, p_rest = y, y_rest
        z, z_rest = None, None
        for sweep in range(SWEEPS):
            last = sweep == SWEEPS - 1
            y_low = y_rest.astype(BF16)
            if sweep > 0:
                z_low = z_rest.astype(BF16)
                p = z * y
                p_rest = z * y_rest + y * z_rest + times(z_low, y_low)
            p_low = p_rest.astype(BF16)
            s = 1.5 - 0.5 * p
            if sweep == 0:
                y_rest = s * y_rest - 0.5 * (y * p_rest + times(y_low, p_low))
                z, z_rest = s, -0.5 * p_rest
                y = s * y
            elif not last:
                both = times(jnp.concatenate([y_low, z_low], axis=0), p_low)
                y_rest = s * y_rest - 0.5 * (y * p_rest + both[:members])
                z_rest = s * z_rest - 0.5 * (z * p_rest + both[members:])
                y, z = s * y, s * z
            else:
                z_rest = s * z_rest - 0.5 * (z * p_rest + times(z_low, p_low))
                z = s * z
        root = (z * eye + z_rest) * lax.rsqrt(frob)
        inner = jnp.sum(root * pull_row, axis=1, keepdims=True)
        shift = jnp.sum(root * inner, axis=0, keepdims=True) * (1.0 / (members - 1))
        blend_ref[pl.ds(pl.multiple_of(b * members, 16), members), :] = (root + shift).astype(BF16)

    def block_group(i, carry):
        for u in range(unroll):
            one_block(i * unroll + u)
        return carry

    lax.fori_loop(0, blocks // unroll, block_group, 0)


def blends(rows, tapers, left, own, right, members):
    blocks, neighbours = rows.shape
    return pl.pallas_call(
        functools.partial(
            blend_kernel, members=members, neighbours=neighbours, blocks=blocks, unroll=4
        ),
        out_shape=jax.ShapeDtypeStruct((blocks * members, LANES), BF16),
        in_specs=[smem(), smem(), vmem(), vmem(), vmem()],
        out_specs=vmem(),
        scratch_shapes=[
            pltpu.VMEM((left.shape[0] + own.shape[0] + right.shape[0], LANES), F32)
        ],
        compiler_params=params(),
        cost_estimate=pl.CostEstimate(
            flops=blocks * 24 * members * members * LANES,
            bytes_accessed=4 * own.shape[0] * LANES * 4,
            transcendentals=0,
        ),
        name="blends",
    )(rows.reshape(-1), tapers.reshape(-1), left, own, right)


def apply_kernel(mem_ref, *refs, groups, share, blocks, width, unroll):
    parts = refs[:groups]
    blend_ref = refs[groups]
    outs = refs[groups + 1 : 2 * groups + 1]
    center_ref, rows_ref = refs[2 * groups + 1 :]
    members = groups * share
    tiles = width // LANES
    mem = mem_ref[0]
    zero = jnp.zeros((blocks, width), F32)
    center = zero
    for d in range(groups):
        center = lax.fori_loop(
            0, share, lambda k, acc, part=parts[d]: acc + part[k].astype(F32), center, unroll=4
        )
    center = center * (1.0 / members)
    center_ref[...] = center
    for d in range(groups):
        base = (mem ^ d) * (share * blocks)

        def perturb(k, carry, part=parts[d], base=base):
            value = (part[k].astype(F32) - center_ref[...]).astype(BF16).astype(F32)
            start = pl.multiple_of(base + k * blocks, 8)
            for t in range(tiles):
                rows_ref[t, pl.ds(start, blocks), :] = value[:, t * LANES : (t + 1) * LANES]
            return carry

        lax.fori_loop(0, share, perturb, 0, unroll=4)

    pad_depth = jnp.zeros((LANES - members, width), BF16)

    def block_group(i, carry):
        for u in range(unroll):
            b = i * unroll + u
            at = pl.ds(b, members, stride=blocks)
            anomalies = jnp.concatenate([rows_ref[t, at, :] for t in range(tiles)], axis=1)
            mixed = jnp.dot(
                blend_ref[pl.ds(pl.multiple_of(b * members, 16), members), :],
                jnp.concatenate([anomalies.astype(BF16), pad_depth], axis=0),
                preferred_element_type=F32,
            )
            for t in range(tiles):
                rows_ref[t, at, :] = mixed[:, t * LANES : (t + 1) * LANES]
        return carry

    lax.fori_loop(0, blocks // unroll, block_group, 0)

    for d in range(groups):
        base = (mem ^ d) * (share * blocks)

        def finish(k, carry, out=outs[d], base=base):
            start = pl.multiple_of(base + k * blocks, 8)
            mixed = jnp.concatenate(
                [rows_ref[t, pl.ds(start, blocks), :] for t in range(tiles)], axis=1
            )
            out[k] = (center_ref[...] + mixed).astype(BF16)
            return carry

        lax.fori_loop(0, share, finish, 0, unroll=4)


def apply_blend(mem, parts, blend):
    groups = len(parts)
    share, blocks, width = parts[0].shape
    members = groups * share
    part = jax.ShapeDtypeStruct((share, blocks, width), BF16)
    return pl.pallas_call(
        functools.partial(
            apply_kernel, groups=groups, share=share, blocks=blocks, width=width, unroll=4
        ),
        out_shape=(part,) * groups,
        in_specs=[smem()] + [vmem()] * (groups + 1),
        out_specs=(vmem(),) * groups,
        scratch_shapes=[
            pltpu.VMEM((blocks, width), F32),
            pltpu.VMEM((width // LANES, members * blocks, LANES), F32),
        ],
        compiler_params=params(),
        cost_estimate=pl.CostEstimate(
            flops=2 * blocks * members * LANES * width,
            bytes_accessed=2 * members * blocks * width * 2,
            transcendentals=0,
        ),
        name="apply_blend",
    )(mem, *parts, blend)


def taper_of(offset):
    ratio = offset.astype(F32) / RADIUS
    return 1.0 / (1.0 + ratio * ratio)


def on_device(
    prior_fields,
    scaled_sensor_spread,
    measured_misfit,
    inverse_error_variance,
    active_sensor_number,
    adjacent_tiles,
):
    groups = lax.axis_size("mem")
    belts = lax.axis_size("lon")
    share, lon_rows, width = scaled_sensor_spread.shape
    members = groups * share
    half = members // 2
    total_blocks = lon_rows * belts
    blocks = lon_rows // groups
    assert groups & (groups - 1) == 0 and blocks == RADIUS
    mem = lax.axis_index("mem")
    lon = lax.axis_index("lon")
    flip = (lon % 2) * (groups - 1)
    mine = mem ^ flip
    peers = [[(i, i ^ d) for i in range(groups)] for d in range(groups)]
    far_first = sorted(range(1, groups), key=lambda d: (d < groups // 2, d))

    def holder(g):
        belt, q = divmod(g % (belts * groups), groups)
        return (q ^ ((belt % 2) * (groups - 1))) * belts + belt

    ring = range(belts * groups)
    forward = [(holder(g), holder(g + 1)) for g in ring]
    backward = [(holder(g), holder(g - 1)) for g in ring]

    def piece(x, d):
        return lax.dynamic_slice_in_dim(x, ((mem ^ d) ^ flip) * blocks, blocks, 1)

    def gathered(x):
        parts = {d: lax.ppermute(piece(x, d), "mem", peers[d]) for d in far_first}
        parts[0] = piece(x, 0)
        return [parts[d] for d in range(groups)]

    def own_rows(x):
        return lax.dynamic_slice_in_dim(x, mine * blocks, blocks, 0)

    mem_scalar = mem.astype(jnp.int32).reshape(1)
    slot_ids = jnp.arange(width, dtype=jnp.int32)
    live = (slot_ids[None, :] < own_rows(active_sensor_number)[:, None]).astype(F32)
    obs_scale = jnp.sqrt(own_rows(inverse_error_variance) * live)
    weighted = own_rows(measured_misfit) * obs_scale
    local_ids = jnp.arange(blocks, dtype=jnp.int32)
    block_ids = lon * lon_rows + mine * blocks + local_ids
    offset_raw = jnp.mod(own_rows(adjacent_tiles) - block_ids[:, None], total_blocks)
    offset = jnp.where(offset_raw > total_blocks // 2, offset_raw - total_blocks, offset_raw)
    window_rows = (local_ids[:, None] + RADIUS + offset) * half
    tapers = taper_of(offset)

    spread_parts = gathered(scaled_sensor_spread)
    field_parts = gathered(prior_fields)
    own, send = packed_grams(mem_scalar, spread_parts, obs_scale, weighted)
    left = lax.ppermute(send, ("mem", "lon"), forward)
    right = lax.ppermute(send, ("mem", "lon"), backward)
    blend = blends(window_rows, tapers, left, own, right, members)
    out_parts = apply_blend(mem_scalar, field_parts, blend)
    result = jnp.zeros(prior_fields.shape, BF16)
    result = lax.dynamic_update_slice_in_dim(result, out_parts[0], mine * blocks, 1)
    for d in reversed(far_first):
        came = lax.ppermute(out_parts[d], "mem", peers[d])
        result = lax.dynamic_update_slice_in_dim(result, came, ((mem ^ d) ^ flip) * blocks, 1)
    return result


def solution(mesh):
    return jax.shard_map(
        on_device,
        mesh=mesh,
        in_specs=(
            P("mem", "lon", None),
            P("mem", "lon", None),
            P("lon", None),
            P("lon", None),
            P("lon"),
            P("lon", None),
        ),
        out_specs=P("mem", "lon", None),
        check_vma=False,
    )
```

```python
import functools

import jax
import jax.numpy as jnp
from jax import lax
from jax.experimental import pallas as pl
from jax.experimental.pallas import tpu as pltpu
from jax.sharding import PartitionSpec as P

RADIUS = 48
SWEEPS = 5
LANES = 128
F32 = jnp.float32
BF16 = jnp.bfloat16
VMEM_BYTES = 56 * 1024 * 1024


def vmem():
    return pl.BlockSpec(memory_space=pltpu.VMEM)


def smem():
    return pl.BlockSpec(memory_space=pltpu.SMEM)


def params():
    return pltpu.CompilerParams(vmem_limit_bytes=VMEM_BYTES)


def gram_kernel(mem_ref, *refs, groups, share, blocks, width, unroll):
    parts = refs[:groups]
    scale_ref, weight_ref, own_ref, send_ref, rows_ref = refs[groups:]
    members = groups * share
    half = members // 2
    tiles = width // LANES
    mem = mem_ref[0]
    scale = scale_ref[...]
    for d in range(groups):
        base = (mem ^ d) * (share * blocks)

        def scale_member(k, carry, part=parts[d], base=base):
            value = (part[k].astype(F32) * scale).astype(BF16).astype(F32)
            start = pl.multiple_of(base + k * blocks, 8)
            for t in range(tiles):
                rows_ref[t, pl.ds(start, blocks), :] = value[:, t * LANES : (t + 1) * LANES]
            return carry

        lax.fori_loop(0, share, scale_member, 0, unroll=4)

    lane = lax.broadcasted_iota(jnp.int32, (half, LANES), 1)
    pull_lane = members + half
    from_top = (lane < members) | (lane == pull_lane) | (lane == pull_lane + 2)
    spare = LANES - pull_lane

    def block_group(i, carry):
        for u in range(unroll):
            b = i * unroll + u
            spread = jnp.concatenate(
                [rows_ref[t, pl.ds(b, members, stride=blocks), :] for t in range(tiles)], axis=1
            )
            weights = jnp.broadcast_to(weight_ref[pl.ds(b, 1), :], (spare, width))
            right = jnp.concatenate([spread, spread[half:], weights], axis=0).astype(BF16)
            product = lax.dot_general(
                spread.astype(BF16), right, (((1,), (1,)), ((), ())), preferred_element_type=F32
            )
            packed = jnp.where(from_top, product[:half], product[half:])
            own_ref[pl.ds(pl.multiple_of(b * half, 8), half), :] = packed
        return carry

    lax.fori_loop(0, blocks // unroll, block_group, 0)

    step = 2 * half
    lane2 = lax.broadcasted_iota(jnp.int32, (step, LANES), 1)

    def finish(i, carry):
        at = pl.ds(pl.multiple_of(i * step, 16), step)
        value = own_ref[at, :]
        low = value - value.astype(BF16).astype(F32)
        is_low = lane2 >= pull_lane + 2
        send_ref[at, :] = jnp.where(is_low, low, value).astype(BF16)
        own_ref[at, :] = jnp.where(is_low, 0.0, value)
        return carry

    lax.fori_loop(0, blocks // 2, finish, 0, unroll=2)


def packed_grams(mem, parts, scale, weighted):
    groups = len(parts)
    share, blocks, width = parts[0].shape
    members = groups * share
    half = members // 2
    assert members + half + 4 <= LANES and half % 8 == 0
    flat = (blocks * half, LANES)
    return pl.pallas_call(
        functools.partial(
            gram_kernel, groups=groups, share=share, blocks=blocks, width=width, unroll=4
        ),
        out_shape=(jax.ShapeDtypeStruct(flat, F32), jax.ShapeDtypeStruct(flat, BF16)),
        in_specs=[smem()] + [vmem()] * (groups + 2),
        out_specs=(vmem(), vmem()),
        scratch_shapes=[pltpu.VMEM((width // LANES, members * blocks, LANES), F32)],
        compiler_params=params(),
        cost_estimate=pl.CostEstimate(
            flops=2 * blocks * members * width * LANES,
            bytes_accessed=members * blocks * width * 2,
            transcendentals=0,
        ),
        name="packed_grams",
    )(mem, *parts, scale, weighted)


def blend_kernel(
    row_ref, taper_ref, left_ref, own_ref, right_ref, blend_ref, window_ref, *, members, neighbours, blocks, unroll
):
    half = members // 2
    pull_lane = members + half
    halo = left_ref.shape[0]
    count = own_ref.shape[0]
    window_ref[pl.ds(0, halo), :] = left_ref[...].astype(F32)
    window_ref[pl.ds(halo, count), :] = own_ref[...]
    window_ref[pl.ds(halo + count, halo), :] = right_ref[...].astype(F32)
    full = (members, LANES)
    lane = lax.broadcasted_iota(jnp.int32, full, 1)
    row = lax.broadcasted_iota(jnp.int32, full, 0)
    eye = (lane == row).astype(F32)
    in_matrix = lax.broadcasted_iota(jnp.int32, (1, LANES), 1) < members
    share_row = jnp.where(in_matrix, 1.0 / (members - 1), 0.0)
    left_half = lax.broadcasted_iota(jnp.int32, (half, LANES), 1) < half
    pad_rows = jnp.zeros((LANES - half, LANES), F32)
    pad_depth = jnp.zeros((LANES - members, LANES), BF16)

    def total(x):
        return jnp.sum(jnp.sum(x, axis=0, keepdims=True), axis=1, keepdims=True)

    def times(lhs, rhs):
        return jnp.dot(
            lhs, jnp.concatenate([rhs, pad_depth], axis=0), preferred_element_type=F32
        )

    def localized_sum(b):
        packed = None
        for n in range(neighbours):
            start = pl.multiple_of(row_ref[b * neighbours + n], 8)
            term = taper_ref[b * neighbours + n] * window_ref[pl.ds(start, half), :]
            packed = term if packed is None else packed + term
        turned = jnp.concatenate([packed, pad_rows], axis=0).T
        low_rows = jnp.where(
            left_half, turned[half:members], pltpu.roll(packed, LANES - half, axis=1)
        )
        pull = turned[pull_lane : pull_lane + 8]
        pull_row = (pull[0:1] + pull[2:3]) + pltpu.roll(pull[1:2] + pull[3:4], half, axis=1)
        return jnp.concatenate([packed, low_rows], axis=0) * share_row, pull_row

    def block_group(i, carry):
        group = range(unroll)
        ids = [i * unroll + u for u in group]
        sums = [localized_sum(b) for b in ids]
        gram = [g for g, _ in sums]
        trace = [total(g * eye) for g in gram]
        square = [total(g * g) for g in gram]
        frob2 = [square[u] + 2.0 * trace[u] + float(members) for u in group]
        inv = [lax.rsqrt(f) for f in frob2]
        mean = [t * (1.0 / members) for t in trace]
        y = [(1.0 + mean[u]) * inv[u] for u in group]
        y_rest = [(gram[u] - mean[u] * eye) * inv[u] for u in group]
        p = [-0.5 * v for v in y]
        p_rest = [-0.5 * v for v in y_rest]
        s = [1.5 + v for v in p]
        y_low = [v.astype(BF16) for v in y_rest]
        p_low = [v.astype(BF16) for v in p_rest]
        prod = [times(y_low[u], p_low[u]) for u in group]
        z = [-0.5 * v for v in s]
        z_rest = [-0.5 * v for v in p_rest]
        y_rest = [(s[u] * y_rest[u] + y[u] * p_rest[u]) + prod[u] for u in group]
        y = [s[u] * y[u] for u in group]
        for sweep in range(1, SWEEPS):
            last = sweep == SWEEPS - 1
            y_low = [v.astype(BF16) for v in y_rest]
            z_low = [v.astype(BF16) for v in z_rest]
            prod = [times(z_low[u], y_low[u]) for u in group]
            p = [z[u] * y[u] for u in group]
            p_rest = [(z[u] * y_rest[u] + y[u] * z_rest[u]) + prod[u] for u in group]
            s = [1.5 + v for v in p]
            p_low = [v.astype(BF16) for v in p_rest]
            if last:
                prod = [times(z_low[u], p_low[u]) for u in group]
                z_rest = [(s[u] * z_rest[u] + z[u] * p_rest[u]) + prod[u] for u in group]
            else:
                prod = [
                    times(jnp.concatenate([y_low[u], z_low[u]], axis=0), p_low[u])
                    for u in group
                ]
                y_rest = [
                    (s[u] * y_rest[u] + y[u] * p_rest[u]) + prod[u][:members] for u in group
                ]
                z_rest = [
                    (s[u] * z_rest[u] + z[u] * p_rest[u]) + prod[u][members:] for u in group
                ]
                y = [s[u] * y[u] for u in group]
            z = [s[u] * z[u] for u in group]
        root = [z[u] * eye + z_rest[u] for u in group]
        norm = [-2.0 * jnp.sqrt(v) for v in inv]
        inner = [
            jnp.sum(root[u] * sums[u][1], axis=1, keepdims=True) for u in group
        ]
        shift = [
            jnp.sum(root[u] * inner[u], axis=0, keepdims=True)
            * (norm[u] * norm[u] * (1.0 / (members - 1)))
            for u in group
        ]
        for u in group:
            at = pl.ds(pl.multiple_of(ids[u] * members, 16), members)
            blend_ref[at, :] = (norm[u] * root[u] + shift[u]).astype(BF16)
        return carry

    lax.fori_loop(0, blocks // unroll, block_group, 0)


def blends(rows, tapers, left, own, right, members):
    blocks, neighbours = rows.shape
    return pl.pallas_call(
        functools.partial(
            blend_kernel, members=members, neighbours=neighbours, blocks=blocks, unroll=12
        ),
        out_shape=jax.ShapeDtypeStruct((blocks * members, LANES), BF16),
        in_specs=[smem(), smem(), vmem(), vmem(), vmem()],
        out_specs=vmem(),
        scratch_shapes=[
            pltpu.VMEM((left.shape[0] + own.shape[0] + right.shape[0], LANES), F32)
        ],
        compiler_params=params(),
        cost_estimate=pl.CostEstimate(
            flops=blocks * 24 * members * members * LANES,
            bytes_accessed=4 * own.shape[0] * LANES * 4,
            transcendentals=0,
        ),
        name="blends",
    )(rows.reshape(-1), tapers.reshape(-1), left, own, right)


def apply_kernel(mem_ref, *refs, groups, share, blocks, width, unroll):
    parts = refs[:groups]
    blend_ref = refs[groups]
    outs = refs[groups + 1 : 2 * groups + 1]
    center_ref, rows_ref = refs[2 * groups + 1 :]
    members = groups * share
    tiles = width // LANES
    mem = mem_ref[0]
    zero = jnp.zeros((blocks, width), F32)
    center = zero
    for d in range(groups):
        center = lax.fori_loop(
            0, share, lambda k, acc, part=parts[d]: acc + part[k].astype(F32), center, unroll=4
        )
    center = center * (1.0 / members)
    center_ref[...] = center
    for d in range(groups):
        base = (mem ^ d) * (share * blocks)

        def perturb(k, carry, part=parts[d], base=base):
            value = (part[k].astype(F32) - center_ref[...]).astype(BF16).astype(F32)
            start = pl.multiple_of(base + k * blocks, 8)
            for t in range(tiles):
                rows_ref[t, pl.ds(start, blocks), :] = value[:, t * LANES : (t + 1) * LANES]
            return carry

        lax.fori_loop(0, share, perturb, 0, unroll=4)

    pad_depth = jnp.zeros((LANES - members, width), BF16)

    def block_group(i, carry):
        for u in range(unroll):
            b = i * unroll + u
            at = pl.ds(b, members, stride=blocks)
            anomalies = jnp.concatenate([rows_ref[t, at, :] for t in range(tiles)], axis=1)
            mixed = jnp.dot(
                blend_ref[pl.ds(pl.multiple_of(b * members, 16), members), :],
                jnp.concatenate([anomalies.astype(BF16), pad_depth], axis=0),
                preferred_element_type=F32,
            )
            for t in range(tiles):
                rows_ref[t, at, :] = mixed[:, t * LANES : (t + 1) * LANES]
        return carry

    lax.fori_loop(0, blocks // unroll, block_group, 0)

    for d in range(groups):
        base = (mem ^ d) * (share * blocks)

        def finish(k, carry, out=outs[d], base=base):
            start = pl.multiple_of(base + k * blocks, 8)
            mixed = jnp.concatenate(
                [rows_ref[t, pl.ds(start, blocks), :] for t in range(tiles)], axis=1
            )
            out[k] = (center_ref[...] + mixed).astype(BF16)
            return carry

        lax.fori_loop(0, share, finish, 0, unroll=4)


def apply_blend(mem, parts, blend):
    groups = len(parts)
    share, blocks, width = parts[0].shape
    members = groups * share
    part = jax.ShapeDtypeStruct((share, blocks, width), BF16)
    return pl.pallas_call(
        functools.partial(
            apply_kernel, groups=groups, share=share, blocks=blocks, width=width, unroll=4
        ),
        out_shape=(part,) * groups,
        in_specs=[smem()] + [vmem()] * (groups + 1),
        out_specs=(vmem(),) * groups,
        scratch_shapes=[
            pltpu.VMEM((blocks, width), F32),
            pltpu.VMEM((width // LANES, members * blocks, LANES), F32),
        ],
        compiler_params=params(),
        cost_estimate=pl.CostEstimate(
            flops=2 * blocks * members * LANES * width,
            bytes_accessed=2 * members * blocks * width * 2,
            transcendentals=0,
        ),
        name="apply_blend",
    )(mem, *parts, blend)


def taper_of(offset):
    ratio = offset.astype(F32) / RADIUS
    return 1.0 / (1.0 + ratio * ratio)


def on_device(
    prior_fields,
    scaled_sensor_spread,
    measured_misfit,
    inverse_error_variance,
    active_sensor_number,
    adjacent_tiles,
):
    groups = lax.axis_size("mem")
    belts = lax.axis_size("lon")
    share, lon_rows, width = scaled_sensor_spread.shape
    members = groups * share
    half = members // 2
    total_blocks = lon_rows * belts
    blocks = lon_rows // groups
    assert groups & (groups - 1) == 0 and blocks == RADIUS
    mem = lax.axis_index("mem")
    lon = lax.axis_index("lon")
    flip = (lon % 2) * (groups - 1)
    mine = mem ^ flip
    peers = [[(i, i ^ d) for i in range(groups)] for d in range(groups)]
    far_first = sorted(range(1, groups), key=lambda d: (d < groups // 2, d))

    def holder(g):
        belt, q = divmod(g % (belts * groups), groups)
        return (q ^ ((belt % 2) * (groups - 1))) * belts + belt

    ring = range(belts * groups)
    forward = [(holder(g), holder(g + 1)) for g in ring]
    backward = [(holder(g), holder(g - 1)) for g in ring]

    def piece(x, d):
        return lax.dynamic_slice_in_dim(x, ((mem ^ d) ^ flip) * blocks, blocks, 1)

    def gathered(x):
        parts = {d: lax.ppermute(piece(x, d), "mem", peers[d]) for d in far_first}
        parts[0] = piece(x, 0)
        return [parts[d] for d in range(groups)]

    def own_rows(x):
        return lax.dynamic_slice_in_dim(x, mine * blocks, blocks, 0)

    mem_scalar = mem.astype(jnp.int32).reshape(1)
    slot_ids = jnp.arange(width, dtype=jnp.int32)
    live = (slot_ids[None, :] < own_rows(active_sensor_number)[:, None]).astype(F32)
    obs_scale = jnp.sqrt(own_rows(inverse_error_variance) * live)
    weighted = own_rows(measured_misfit) * obs_scale
    local_ids = jnp.arange(blocks, dtype=jnp.int32)
    block_ids = lon * lon_rows + mine * blocks + local_ids
    offset_raw = jnp.mod(own_rows(adjacent_tiles) - block_ids[:, None], total_blocks)
    offset = jnp.where(offset_raw > total_blocks // 2, offset_raw - total_blocks, offset_raw)
    window_rows = (local_ids[:, None] + RADIUS + offset) * half
    tapers = taper_of(offset)

    spread_parts = gathered(scaled_sensor_spread)
    field_parts = gathered(prior_fields)
    own, send = packed_grams(mem_scalar, spread_parts, obs_scale, weighted)
    left = lax.ppermute(send, ("mem", "lon"), forward)
    right = lax.ppermute(send, ("mem", "lon"), backward)
    blend = blends(window_rows, tapers, left, own, right, members)
    out_parts = apply_blend(mem_scalar, field_parts, blend)
    result = jnp.zeros(prior_fields.shape, BF16)
    result = lax.dynamic_update_slice_in_dim(result, out_parts[0], mine * blocks, 1)
    for d in reversed(far_first):
        came = lax.ppermute(out_parts[d], "mem", peers[d])
        result = lax.dynamic_update_slice_in_dim(result, came, ((mem ^ d) ^ flip) * blocks, 1)
    return result


def solution(mesh):
    return jax.shard_map(
        on_device,
        mesh=mesh,
        in_specs=(
            P("mem", "lon", None),
            P("mem", "lon", None),
            P("lon", None),
            P("lon", None),
            P("lon"),
            P("lon", None),
        ),
        out_specs=P("mem", "lon", None),
        check_vma=False,
    )
```

```python
import functools

import jax
import jax.numpy as jnp
from jax import lax
from jax.experimental import pallas as pl
from jax.experimental.pallas import tpu as pltpu
from jax.sharding import PartitionSpec as P


RADIUS = 48
SWEEPS = 5
LANES = 128
F32 = jnp.float32
BF16 = jnp.bfloat16
VMEM_BYTES = 56 * 1024 * 1024
CHUNKS = 2
GROUP = 12


def group_of(blocks):
    return max(u for u in range(1, GROUP + 1) if blocks % u == 0)


def vmem():
    return pl.BlockSpec(memory_space=pltpu.VMEM)


def smem():
    return pl.BlockSpec(memory_space=pltpu.SMEM)


def params():
    return pltpu.CompilerParams(vmem_limit_bytes=VMEM_BYTES)


def gram_kernel(mem_ref, *refs, groups, share, blocks, width, unroll, first):
    parts = refs[:groups]
    scale_ref, weight_ref, own_ref, send_ref, rows_ref = refs[groups:]
    members = groups * share
    half = members // 2
    tiles = width // LANES
    mem = mem_ref[0]
    scale = scale_ref[first : first + blocks, :]
    for d in range(groups):
        base = (mem ^ d) * (share * blocks)

        def scale_member(k, carry, part=parts[d], base=base):
            value = (part[k].astype(F32) * scale).astype(BF16).astype(F32)
            start = pl.multiple_of(base + k * blocks, 8)
            for t in range(tiles):
                rows_ref[t, pl.ds(start, blocks), :] = value[:, t * LANES : (t + 1) * LANES]
            return carry

        lax.fori_loop(0, share, scale_member, 0, unroll=4)

    lane = lax.broadcasted_iota(jnp.int32, (half, LANES), 1)
    pull_lane = members + half
    from_top = (lane < members) | (lane == pull_lane) | (lane == pull_lane + 2)
    spare = LANES - pull_lane

    def block_group(i, carry):
        for u in range(unroll):
            b = i * unroll + u
            spread = jnp.concatenate(
                [rows_ref[t, pl.ds(b, members, stride=blocks), :] for t in range(tiles)], axis=1
            )
            weights = jnp.broadcast_to(weight_ref[pl.ds(first + b, 1), :], (spare, width))
            right = jnp.concatenate([spread, spread[half:], weights], axis=0).astype(BF16)
            product = lax.dot_general(
                spread.astype(BF16), right, (((1,), (1,)), ((), ())), preferred_element_type=F32
            )
            packed = jnp.where(from_top, product[:half], product[half:])
            own_ref[pl.ds(pl.multiple_of(b * half, 8), half), :] = packed
        return carry

    lax.fori_loop(0, blocks // unroll, block_group, 0)

    step = 2 * half
    lane2 = lax.broadcasted_iota(jnp.int32, (step, LANES), 1)

    def finish(i, carry):
        at = pl.ds(pl.multiple_of(i * step, 16), step)
        value = own_ref[at, :]
        low = value - value.astype(BF16).astype(F32)
        is_low = lane2 >= pull_lane + 2
        send_ref[at, :] = jnp.where(is_low, low, value).astype(BF16)
        own_ref[at, :] = jnp.where(is_low, 0.0, value)
        return carry

    lax.fori_loop(0, blocks // 2, finish, 0, unroll=2)


def packed_grams(mem, parts, scale, weighted, first):
    groups = len(parts)
    share, blocks, width = parts[0].shape
    members = groups * share
    half = members // 2
    assert members + half + 4 <= LANES and half % 8 == 0
    flat = (blocks * half, LANES)
    return pl.pallas_call(
        functools.partial(
            gram_kernel,
            groups=groups,
            share=share,
            blocks=blocks,
            width=width,
            unroll=group_of(blocks),
            first=first,
        ),
        out_shape=(jax.ShapeDtypeStruct(flat, F32), jax.ShapeDtypeStruct(flat, BF16)),
        in_specs=[smem()] + [vmem()] * (groups + 2),
        out_specs=(vmem(), vmem()),
        scratch_shapes=[pltpu.VMEM((width // LANES, members * blocks, LANES), F32)],
        compiler_params=params(),
        cost_estimate=pl.CostEstimate(
            flops=2 * blocks * members * width * LANES,
            bytes_accessed=members * blocks * width * 2,
            transcendentals=0,
        ),
        name="packed_grams",
    )(mem, *parts, scale, weighted)


def blend_kernel(
    row_ref, taper_ref, *refs, members, neighbours, blocks, unroll, first
):
    *pieces, blend_ref, window_ref = refs
    half = members // 2
    pull_lane = members + half
    filled = 0
    for piece in pieces:
        window_ref[pl.ds(filled, piece.shape[0]), :] = piece[...].astype(F32)
        filled += piece.shape[0]
    full = (members, LANES)
    lane = lax.broadcasted_iota(jnp.int32, full, 1)
    row = lax.broadcasted_iota(jnp.int32, full, 0)
    eye = (lane == row).astype(F32)
    in_matrix = lax.broadcasted_iota(jnp.int32, (1, LANES), 1) < members
    share_row = jnp.where(in_matrix, 1.0 / (members - 1), 0.0)
    left_half = lax.broadcasted_iota(jnp.int32, (half, LANES), 1) < half
    pad_rows = jnp.zeros((LANES - half, LANES), F32)
    pad_depth = jnp.zeros((LANES - members, LANES), BF16)

    def total(x):
        return jnp.sum(jnp.sum(x, axis=0, keepdims=True), axis=1, keepdims=True)

    def times(lhs, rhs):
        return jnp.dot(
            lhs, jnp.concatenate([rhs, pad_depth], axis=0), preferred_element_type=F32
        )

    def localized_sum(b):
        packed = None
        for n in range(neighbours):
            start = pl.multiple_of(row_ref[first + b, n], 8)
            term = taper_ref[first + b, n] * window_ref[pl.ds(start, half), :]
            packed = term if packed is None else packed + term
        turned = jnp.concatenate([packed, pad_rows], axis=0).T
        low_rows = jnp.where(
            left_half, turned[half:members], pltpu.roll(packed, LANES - half, axis=1)
        )
        pull = turned[pull_lane : pull_lane + 8]
        pull_row = (pull[0:1] + pull[2:3]) + pltpu.roll(pull[1:2] + pull[3:4], half, axis=1)
        return jnp.concatenate([packed, low_rows], axis=0) * share_row, pull_row

    def block_group(i, carry):
        group = range(unroll)
        ids = [i * unroll + u for u in group]
        sums = [localized_sum(b) for b in ids]
        gram = [g for g, _ in sums]
        trace = [total(g * eye) for g in gram]
        square = [total(g * g) for g in gram]
        frob2 = [square[u] + 2.0 * trace[u] + float(members) for u in group]
        inv = [lax.rsqrt(f) for f in frob2]
        mean = [t * (1.0 / members) for t in trace]
        y = [(1.0 + mean[u]) * inv[u] for u in group]
        y_rest = [(gram[u] - mean[u] * eye) * inv[u] for u in group]
        p = [-0.5 * v for v in y]
        p_rest = [-0.5 * v for v in y_rest]
        s = [1.5 + v for v in p]
        y_low = [v.astype(BF16) for v in y_rest]
        p_low = [v.astype(BF16) for v in p_rest]
        prod = [times(y_low[u], p_low[u]) for u in group]
        z = [-0.5 * v for v in s]
        z_rest = [-0.5 * v for v in p_rest]
        y_rest = [(s[u] * y_rest[u] + y[u] * p_rest[u]) + prod[u] for u in group]
        y = [s[u] * y[u] for u in group]
        for sweep in range(1, SWEEPS):
            last = sweep == SWEEPS - 1
            y_low = [v.astype(BF16) for v in y_rest]
            z_low = [v.astype(BF16) for v in z_rest]
            prod = [times(z_low[u], y_low[u]) for u in group]
            p = [z[u] * y[u] for u in group]
            p_rest = [(z[u] * y_rest[u] + y[u] * z_rest[u]) + prod[u] for u in group]
            s = [1.5 + v for v in p]
            p_low = [v.astype(BF16) for v in p_rest]
            if last:
                prod = [times(z_low[u], p_low[u]) for u in group]
                z_rest = [(s[u] * z_rest[u] + z[u] * p_rest[u]) + prod[u] for u in group]
            else:
                prod = [
                    times(jnp.concatenate([y_low[u], z_low[u]], axis=0), p_low[u])
                    for u in group
                ]
                y_rest = [
                    (s[u] * y_rest[u] + y[u] * p_rest[u]) + prod[u][:members] for u in group
                ]
                z_rest = [
                    (s[u] * z_rest[u] + z[u] * p_rest[u]) + prod[u][members:] for u in group
                ]
                y = [s[u] * y[u] for u in group]
            z = [s[u] * z[u] for u in group]
        root = [z[u] * eye + z_rest[u] for u in group]
        norm = [-2.0 * jnp.sqrt(v) for v in inv]
        inner = [
            jnp.sum(root[u] * sums[u][1], axis=1, keepdims=True) for u in group
        ]
        shift = [
            jnp.sum(root[u] * inner[u], axis=0, keepdims=True)
            * (norm[u] * norm[u] * (1.0 / (members - 1)))
            for u in group
        ]
        for u in group:
            at = pl.ds(pl.multiple_of(ids[u] * members, 16), members)
            blend_ref[at, :] = (norm[u] * root[u] + shift[u]).astype(BF16)
        return carry

    lax.fori_loop(0, blocks // unroll, block_group, 0)


def blends(rows, tapers, window, members, first, blocks):
    neighbours = rows.shape[1]
    window_rows = sum(piece.shape[0] for piece in window)
    return pl.pallas_call(
        functools.partial(
            blend_kernel,
            members=members,
            neighbours=neighbours,
            blocks=blocks,
            unroll=group_of(blocks),
            first=first,
        ),
        out_shape=jax.ShapeDtypeStruct((blocks * members, LANES), BF16),
        in_specs=[smem(), smem()] + [vmem()] * len(window),
        out_specs=vmem(),
        scratch_shapes=[pltpu.VMEM((window_rows, LANES), F32)],
        compiler_params=params(),
        cost_estimate=pl.CostEstimate(
            flops=blocks * 24 * members * members * LANES,
            bytes_accessed=3 * window_rows * LANES,
            transcendentals=0,
        ),
        name="blends",
    )(rows, tapers, *window)


def apply_kernel(mem_ref, *refs, groups, share, blocks, width, unroll):
    parts = refs[:groups]
    blend_ref = refs[groups]
    outs = refs[groups + 1 : 2 * groups + 1]
    center_ref, rows_ref = refs[2 * groups + 1 :]
    members = groups * share
    tiles = width // LANES
    mem = mem_ref[0]
    zero = jnp.zeros((blocks, width), F32)
    center = zero
    for d in range(groups):
        center = lax.fori_loop(
            0, share, lambda k, acc, part=parts[d]: acc + part[k].astype(F32), center, unroll=4
        )
    center = center * (1.0 / members)
    center_ref[...] = center
    for d in range(groups):
        base = (mem ^ d) * (share * blocks)

        def perturb(k, carry, part=parts[d], base=base):
            value = (part[k].astype(F32) - center_ref[...]).astype(BF16).astype(F32)
            start = pl.multiple_of(base + k * blocks, 8)
            for t in range(tiles):
                rows_ref[t, pl.ds(start, blocks), :] = value[:, t * LANES : (t + 1) * LANES]
            return carry

        lax.fori_loop(0, share, perturb, 0, unroll=4)

    pad_depth = jnp.zeros((LANES - members, width), BF16)

    def block_group(i, carry):
        for u in range(unroll):
            b = i * unroll + u
            at = pl.ds(b, members, stride=blocks)
            anomalies = jnp.concatenate([rows_ref[t, at, :] for t in range(tiles)], axis=1)
            mixed = jnp.dot(
                blend_ref[pl.ds(pl.multiple_of(b * members, 16), members), :],
                jnp.concatenate([anomalies.astype(BF16), pad_depth], axis=0),
                preferred_element_type=F32,
            )
            for t in range(tiles):
                rows_ref[t, at, :] = mixed[:, t * LANES : (t + 1) * LANES]
        return carry

    lax.fori_loop(0, blocks // unroll, block_group, 0)

    for d in range(groups):
        base = (mem ^ d) * (share * blocks)

        def finish(k, carry, out=outs[d], base=base):
            start = pl.multiple_of(base + k * blocks, 8)
            mixed = jnp.concatenate(
                [rows_ref[t, pl.ds(start, blocks), :] for t in range(tiles)], axis=1
            )
            out[k] = (center_ref[...] + mixed).astype(BF16)
            return carry

        lax.fori_loop(0, share, finish, 0, unroll=4)


def apply_blend(mem, parts, blend):
    groups = len(parts)
    share, blocks, width = parts[0].shape
    members = groups * share
    part = jax.ShapeDtypeStruct((share, blocks, width), BF16)
    return pl.pallas_call(
        functools.partial(
            apply_kernel, groups=groups, share=share, blocks=blocks, width=width, unroll=group_of(blocks)
        ),
        out_shape=(part,) * groups,
        in_specs=[smem()] + [vmem()] * (groups + 1),
        out_specs=(vmem(),) * groups,
        scratch_shapes=[
            pltpu.VMEM((blocks, width), F32),
            pltpu.VMEM((width // LANES, members * blocks, LANES), F32),
        ],
        compiler_params=params(),
        cost_estimate=pl.CostEstimate(
            flops=2 * blocks * members * LANES * width,
            bytes_accessed=2 * members * blocks * width * 2,
            transcendentals=0,
        ),
        name="apply_blend",
    )(mem, *parts, blend)


def taper_of(offset):
    ratio = offset.astype(F32) / RADIUS
    return 1.0 / (1.0 + ratio * ratio)


def on_device(
    prior_fields,
    scaled_sensor_spread,
    measured_misfit,
    inverse_error_variance,
    active_sensor_number,
    adjacent_tiles,
):
    groups = lax.axis_size("mem")
    belts = lax.axis_size("lon")
    share, lon_rows, width = scaled_sensor_spread.shape
    members = groups * share
    half = members // 2
    total_blocks = lon_rows * belts
    blocks = lon_rows // groups
    assert groups & (groups - 1) == 0 and blocks == RADIUS
    mem = lax.axis_index("mem")
    lon = lax.axis_index("lon")
    flip = (lon % 2) * (groups - 1)
    mine = mem ^ flip
    peers = [[(i, i ^ d) for i in range(groups)] for d in range(groups)]
    far_first = sorted(range(1, groups), key=lambda d: (d < groups // 2, d))

    def holder(g):
        belt, q = divmod(g % (belts * groups), groups)
        return (q ^ ((belt % 2) * (groups - 1))) * belts + belt

    ring = range(belts * groups)
    forward = [(holder(g), holder(g + 1)) for g in ring]
    backward = [(holder(g), holder(g - 1)) for g in ring]

    size = blocks // CHUNKS
    chunks = range(CHUNKS)
    last = None

    def piece(x, d, c):
        nonlocal last
        if last is not None:
            x, _ = lax.optimization_barrier((x, last))
        start = ((mem ^ d) ^ flip) * blocks + c * size
        last = lax.dynamic_slice_in_dim(x, start, size, 1)
        return last

    def own_rows(x):
        return lax.dynamic_slice_in_dim(x, mine * blocks, blocks, 0)

    def exchanged(x, c):
        parts = {d: lax.ppermute(piece(x, d, c), "mem", peers[d]) for d in far_first}
        parts[0] = piece(x, 0, c)
        return [parts[d] for d in range(groups)]

    spread_parts = [exchanged(scaled_sensor_spread, c) for c in chunks]
    field_parts = [exchanged(prior_fields, c) for c in chunks]

    mem_scalar = mem.astype(jnp.int32).reshape(1)
    slot_ids = jnp.arange(width, dtype=jnp.int32)
    live = (slot_ids[None, :] < own_rows(active_sensor_number)[:, None]).astype(F32)
    obs_scale = jnp.sqrt(own_rows(inverse_error_variance) * live)
    weighted = own_rows(measured_misfit) * obs_scale
    local_ids = jnp.arange(blocks, dtype=jnp.int32)
    block_ids = lon * lon_rows + mine * blocks + local_ids
    offset_raw = jnp.mod(own_rows(adjacent_tiles) - block_ids[:, None], total_blocks)
    offset = jnp.where(offset_raw > total_blocks // 2, offset_raw - total_blocks, offset_raw)
    window_rows = (local_ids[:, None] % size + RADIUS + offset) * half
    tapers = taper_of(offset)

    left, own, right = [], [], []
    for c in chunks:
        here, packed = packed_grams(
            mem_scalar, spread_parts[c], obs_scale, weighted, c * size
        )
        own.append(here)
        left.append(lax.ppermute(packed, ("mem", "lon"), forward))
        right.append(lax.ppermute(packed, ("mem", "lon"), backward))
    window = left + own + right

    came = []
    for c in chunks:
        blend = blends(window_rows, tapers, window[c : c + 2 * CHUNKS + 1], members, c * size, size)
        out_parts = apply_blend(mem_scalar, field_parts[c], blend)
        came.append((0, c, out_parts[0]))
        for d in far_first:
            came.append((d, c, lax.ppermute(out_parts[d], "mem", peers[d])))
    result = jnp.zeros(prior_fields.shape, BF16)
    for d, c, part in sorted(came, key=lambda item: (item[1], item[0] > 0, item[0] >= groups // 2)):
        start = ((mem ^ d) ^ flip) * blocks + c * size
        result = lax.dynamic_update_slice_in_dim(result, part, start, 1)
    return result


def solution(mesh):
    return jax.shard_map(
        on_device,
        mesh=mesh,
        in_specs=(
            P("mem", "lon", None),
            P("mem", "lon", None),
            P("lon", None),
            P("lon", None),
            P("lon"),
            P("lon", None),
        ),
        out_specs=P("mem", "lon", None),
        check_vma=False,
    )
```

```python
import functools

import jax
import jax.numpy as jnp
from jax import lax
from jax.experimental import pallas as pl
from jax.experimental.pallas import tpu as pltpu
from jax.sharding import PartitionSpec as P


RADIUS = 48
SWEEPS = 5
LANES = 128
F32 = jnp.float32
BF16 = jnp.bfloat16
VMEM_BYTES = 16 * 1024 * 1024
CHUNKS = 2
GROUP = 12
PAD = 1


def group_of(blocks):
    return max(u for u in range(1, GROUP + 1) if blocks % u == 0)


def vmem():
    return pl.BlockSpec(memory_space=pltpu.VMEM)


def smem():
    return pl.BlockSpec(memory_space=pltpu.SMEM)


def params():
    return pltpu.CompilerParams(vmem_limit_bytes=VMEM_BYTES)


def gram_kernel(mem_ref, *refs, groups, share, blocks, width, unroll, first):
    parts = refs[:groups]
    scale_ref, weight_ref, own_ref, send_ref, rows_ref = refs[groups:]
    members = groups * share
    half = members // 2
    tiles = width // LANES
    pitch = rows_ref.shape[1] // members
    mem = mem_ref[0]
    scale = scale_ref[first : first + blocks, :]
    for d in range(groups):
        base = (mem ^ d) * (share * pitch)

        def scale_member(k, carry, part=parts[d], base=base):
            value = (part[k].astype(F32) * scale).astype(BF16).astype(F32)
            start = base + k * pitch
            for t in range(tiles):
                rows_ref[t, pl.ds(start, blocks), :] = value[:, t * LANES : (t + 1) * LANES]
            return carry

        lax.fori_loop(0, share, scale_member, 0, unroll=4)

    lane = lax.broadcasted_iota(jnp.int32, (half, LANES), 1)
    pull_lane = members + half
    from_top = (lane < members) | (lane == pull_lane) | (lane == pull_lane + 2)
    spare = LANES - pull_lane

    def block_group(i, carry):
        for u in range(unroll):
            b = i * unroll + u
            spread = jnp.concatenate(
                [rows_ref[t, pl.ds(b, members, stride=pitch), :] for t in range(tiles)], axis=1
            )
            weights = jnp.broadcast_to(weight_ref[pl.ds(first + b, 1), :], (spare, width))
            right = jnp.concatenate([spread, spread[half:], weights], axis=0).astype(BF16)
            product = lax.dot_general(
                spread.astype(BF16), right, (((1,), (1,)), ((), ())), preferred_element_type=F32
            )
            packed = jnp.where(from_top, product[:half], product[half:])
            own_ref[pl.ds(pl.multiple_of(b * half, 8), half), :] = packed
        return carry

    lax.fori_loop(0, blocks // unroll, block_group, 0)

    step = 2 * half
    lane2 = lax.broadcasted_iota(jnp.int32, (step, LANES), 1)

    def finish(i, carry):
        at = pl.ds(pl.multiple_of(i * step, 16), step)
        value = own_ref[at, :]
        low = value - value.astype(BF16).astype(F32)
        is_low = lane2 >= pull_lane + 2
        send_ref[at, :] = jnp.where(is_low, low, value).astype(BF16)
        own_ref[at, :] = jnp.where(is_low, 0.0, value)
        return carry

    lax.fori_loop(0, blocks // 2, finish, 0, unroll=2)


def packed_grams(mem, parts, scale, weighted, first):
    groups = len(parts)
    share, blocks, width = parts[0].shape
    members = groups * share
    half = members // 2
    assert members + half + 4 <= LANES and half % 8 == 0
    flat = (blocks * half, LANES)
    return pl.pallas_call(
        functools.partial(
            gram_kernel,
            groups=groups,
            share=share,
            blocks=blocks,
            width=width,
            unroll=group_of(blocks),
            first=first,
        ),
        out_shape=(jax.ShapeDtypeStruct(flat, F32), jax.ShapeDtypeStruct(flat, BF16)),
        in_specs=[smem()] + [vmem()] * (groups + 2),
        out_specs=(vmem(), vmem()),
        scratch_shapes=[pltpu.VMEM((width // LANES, members * (blocks + PAD), LANES), F32)],
        compiler_params=params(),
        cost_estimate=pl.CostEstimate(
            flops=2 * blocks * members * width * LANES,
            bytes_accessed=members * blocks * width * 2,
            transcendentals=0,
        ),
        name="packed_grams",
    )(mem, *parts, scale, weighted)


def blend_kernel(
    row_ref, taper_ref, *refs, members, neighbours, blocks, unroll, first
):
    *pieces, blend_ref, window_ref = refs
    half = members // 2
    pull_lane = members + half
    filled = 0
    for piece in pieces:
        window_ref[pl.ds(filled, piece.shape[0]), :] = piece[...].astype(F32)
        filled += piece.shape[0]
    full = (members, LANES)
    lane = lax.broadcasted_iota(jnp.int32, full, 1)
    row = lax.broadcasted_iota(jnp.int32, full, 0)
    eye = (lane == row).astype(F32)
    in_matrix = lax.broadcasted_iota(jnp.int32, (1, LANES), 1) < members
    share_row = jnp.where(in_matrix, 1.0 / (members - 1), 0.0)
    left_half = lax.broadcasted_iota(jnp.int32, (half, LANES), 1) < half
    pad_rows = jnp.zeros((LANES - half, LANES), F32)
    pad_depth = jnp.zeros((LANES - members, LANES), BF16)

    def total(x):
        return jnp.sum(jnp.sum(x, axis=0, keepdims=True), axis=1, keepdims=True)

    def times(lhs, rhs):
        return jnp.dot(
            lhs, jnp.concatenate([rhs, pad_depth], axis=0), preferred_element_type=F32
        )

    def localized_sum(b):
        packed = None
        for n in range(neighbours):
            start = pl.multiple_of(row_ref[first + b, n], 8)
            term = taper_ref[first + b, n] * window_ref[pl.ds(start, half), :]
            packed = term if packed is None else packed + term
        turned = jnp.concatenate([packed, pad_rows], axis=0).T
        low_rows = jnp.where(
            left_half, turned[half:members], pltpu.roll(packed, LANES - half, axis=1)
        )
        pull = turned[pull_lane : pull_lane + 8]
        pull_row = (pull[0:1] + pull[2:3]) + pltpu.roll(pull[1:2] + pull[3:4], half, axis=1)
        return jnp.concatenate([packed, low_rows], axis=0) * share_row, pull_row

    def block_group(i, carry):
        group = range(unroll)
        ids = [i * unroll + u for u in group]
        sums = [localized_sum(b) for b in ids]
        gram = [g for g, _ in sums]
        trace = [total(g * eye) for g in gram]
        square = [total(g * g) for g in gram]
        frob2 = [square[u] + 2.0 * trace[u] + float(members) for u in group]
        inv = [lax.rsqrt(f) for f in frob2]
        mean = [t * (1.0 / members) for t in trace]
        y = [(1.0 + mean[u]) * inv[u] for u in group]
        y_rest = [(gram[u] - mean[u] * eye) * inv[u] for u in group]
        p = [-0.5 * v for v in y]
        p_rest = [-0.5 * v for v in y_rest]
        s = [1.5 + v for v in p]
        y_low = [v.astype(BF16) for v in y_rest]
        p_low = [v.astype(BF16) for v in p_rest]
        prod = [times(y_low[u], p_low[u]) for u in group]
        z = [-0.5 * v for v in s]
        z_rest = [-0.5 * v for v in p_rest]
        y_rest = [(s[u] * y_rest[u] + y[u] * p_rest[u]) + prod[u] for u in group]
        y = [s[u] * y[u] for u in group]
        for sweep in range(1, SWEEPS):
            last = sweep == SWEEPS - 1
            y_low = [v.astype(BF16) for v in y_rest]
            z_low = [v.astype(BF16) for v in z_rest]
            prod = [times(z_low[u], y_low[u]) for u in group]
            p = [z[u] * y[u] for u in group]
            p_rest = [(z[u] * y_rest[u] + y[u] * z_rest[u]) + prod[u] for u in group]
            s = [1.5 + v for v in p]
            p_low = [v.astype(BF16) for v in p_rest]
            if last:
                prod = [times(z_low[u], p_low[u]) for u in group]
                z_rest = [(s[u] * z_rest[u] + z[u] * p_rest[u]) + prod[u] for u in group]
            else:
                prod = [
                    times(jnp.concatenate([y_low[u], z_low[u]], axis=0), p_low[u])
                    for u in group
                ]
                y_rest = [
                    (s[u] * y_rest[u] + y[u] * p_rest[u]) + prod[u][:members] for u in group
                ]
                z_rest = [
                    (s[u] * z_rest[u] + z[u] * p_rest[u]) + prod[u][members:] for u in group
                ]
                y = [s[u] * y[u] for u in group]
            z = [s[u] * z[u] for u in group]
        root = [z[u] * eye + z_rest[u] for u in group]
        norm = [-2.0 * jnp.sqrt(v) for v in inv]
        inner = [
            jnp.sum(root[u] * sums[u][1], axis=1, keepdims=True) for u in group
        ]
        shift = [
            jnp.sum(root[u] * inner[u], axis=0, keepdims=True)
            * (norm[u] * norm[u] * (1.0 / (members - 1)))
            for u in group
        ]
        for u in group:
            at = pl.ds(pl.multiple_of(ids[u] * members, 16), members)
            blend_ref[at, :] = (norm[u] * root[u] + shift[u]).astype(BF16)
        return carry

    lax.fori_loop(0, blocks // unroll, block_group, 0)


def blends(rows, tapers, window, members, first, blocks):
    neighbours = rows.shape[1]
    window_rows = sum(piece.shape[0] for piece in window)
    return pl.pallas_call(
        functools.partial(
            blend_kernel,
            members=members,
            neighbours=neighbours,
            blocks=blocks,
            unroll=group_of(blocks),
            first=first,
        ),
        out_shape=jax.ShapeDtypeStruct((blocks * members, LANES), BF16),
        in_specs=[smem(), smem()] + [vmem()] * len(window),
        out_specs=vmem(),
        scratch_shapes=[pltpu.VMEM((window_rows, LANES), F32)],
        compiler_params=params(),
        cost_estimate=pl.CostEstimate(
            flops=blocks * 24 * members * members * LANES,
            bytes_accessed=3 * window_rows * LANES,
            transcendentals=0,
        ),
        name="blends",
    )(rows, tapers, *window)


def apply_kernel(mem_ref, *refs, groups, share, blocks, width, unroll):
    parts = refs[:groups]
    blend_ref = refs[groups]
    outs = refs[groups + 1 : 2 * groups + 1]
    center_ref, rows_ref = refs[2 * groups + 1 :]
    members = groups * share
    tiles = width // LANES
    pitch = rows_ref.shape[1] // members
    mem = mem_ref[0]
    zero = jnp.zeros((blocks, width), F32)
    center = zero
    for d in range(groups):
        center = lax.fori_loop(
            0, share, lambda k, acc, part=parts[d]: acc + part[k].astype(F32), center, unroll=4
        )
    center = center * (1.0 / members)
    center_ref[...] = center
    for d in range(groups):
        base = (mem ^ d) * (share * pitch)

        def perturb(k, carry, part=parts[d], base=base):
            value = (part[k].astype(F32) - center_ref[...]).astype(BF16).astype(F32)
            start = base + k * pitch
            for t in range(tiles):
                rows_ref[t, pl.ds(start, blocks), :] = value[:, t * LANES : (t + 1) * LANES]
            return carry

        lax.fori_loop(0, share, perturb, 0, unroll=4)

    pad_depth = jnp.zeros((LANES - members, width), BF16)

    def block_group(i, carry):
        for u in range(unroll):
            b = i * unroll + u
            at = pl.ds(b, members, stride=pitch)
            anomalies = jnp.concatenate([rows_ref[t, at, :] for t in range(tiles)], axis=1)
            mixed = jnp.dot(
                blend_ref[pl.ds(pl.multiple_of(b * members, 16), members), :],
                jnp.concatenate([anomalies.astype(BF16), pad_depth], axis=0),
                preferred_element_type=F32,
            )
            for t in range(tiles):
                rows_ref[t, at, :] = mixed[:, t * LANES : (t + 1) * LANES]
        return carry

    lax.fori_loop(0, blocks // unroll, block_group, 0)

    for d in range(groups):
        base = (mem ^ d) * (share * pitch)

        def finish(k, carry, out=outs[d], base=base):
            start = base + k * pitch
            mixed = jnp.concatenate(
                [rows_ref[t, pl.ds(start, blocks), :] for t in range(tiles)], axis=1
            )
            out[k] = (center_ref[...] + mixed).astype(BF16)
            return carry

        lax.fori_loop(0, share, finish, 0, unroll=4)


def apply_blend(mem, parts, blend):
    groups = len(parts)
    share, blocks, width = parts[0].shape
    members = groups * share
    part = jax.ShapeDtypeStruct((share, blocks, width), BF16)
    return pl.pallas_call(
        functools.partial(
            apply_kernel, groups=groups, share=share, blocks=blocks, width=width, unroll=group_of(blocks)
        ),
        out_shape=(part,) * groups,
        in_specs=[smem()] + [vmem()] * (groups + 1),
        out_specs=(vmem(),) * groups,
        scratch_shapes=[
            pltpu.VMEM((blocks, width), F32),
            pltpu.VMEM((width // LANES, members * (blocks + PAD), LANES), F32),
        ],
        compiler_params=params(),
        cost_estimate=pl.CostEstimate(
            flops=2 * blocks * members * LANES * width,
            bytes_accessed=2 * members * blocks * width * 2,
            transcendentals=0,
        ),
        name="apply_blend",
    )(mem, *parts, blend)


def taper_of(offset):
    ratio = offset.astype(F32) / RADIUS
    return 1.0 / (1.0 + ratio * ratio)


def on_device(
    prior_fields,
    scaled_sensor_spread,
    measured_misfit,
    inverse_error_variance,
    active_sensor_number,
    adjacent_tiles,
):
    groups = lax.axis_size("mem")
    belts = lax.axis_size("lon")
    share, lon_rows, width = scaled_sensor_spread.shape
    members = groups * share
    half = members // 2
    total_blocks = lon_rows * belts
    blocks = lon_rows // groups
    assert groups & (groups - 1) == 0 and blocks == RADIUS
    mem = lax.axis_index("mem")
    lon = lax.axis_index("lon")
    flip = (lon % 2) * (groups - 1)
    mine = mem ^ flip
    peers = [[(i, i ^ d) for i in range(groups)] for d in range(groups)]
    far_first = sorted(range(1, groups), key=lambda d: (d < groups // 2, d))

    def holder(g):
        belt, q = divmod(g % (belts * groups), groups)
        return (q ^ ((belt % 2) * (groups - 1))) * belts + belt

    ring = range(belts * groups)
    forward = [(holder(g), holder(g + 1)) for g in ring]
    backward = [(holder(g), holder(g - 1)) for g in ring]

    size = blocks // CHUNKS
    chunks = range(CHUNKS)
    last = None

    def piece(x, d, c):
        nonlocal last
        if last is not None:
            x, _ = lax.optimization_barrier((x, last))
        start = ((mem ^ d) ^ flip) * blocks + c * size
        last = lax.dynamic_slice_in_dim(x, start, size, 1)
        return last

    def own_rows(x):
        return lax.dynamic_slice_in_dim(x, mine * blocks, blocks, 0)

    def exchanged(x, c):
        parts = {d: lax.ppermute(piece(x, d, c), "mem", peers[d]) for d in far_first}
        parts[0] = piece(x, 0, c)
        return [parts[d] for d in range(groups)]

    spread_parts = [exchanged(scaled_sensor_spread, c) for c in chunks]
    field_parts = [exchanged(prior_fields, c) for c in chunks]

    mem_scalar = mem.astype(jnp.int32).reshape(1)
    slot_ids = jnp.arange(width, dtype=jnp.int32)
    live = (slot_ids[None, :] < own_rows(active_sensor_number)[:, None]).astype(F32)
    obs_scale = jnp.sqrt(own_rows(inverse_error_variance) * live)
    weighted = own_rows(measured_misfit) * obs_scale
    local_ids = jnp.arange(blocks, dtype=jnp.int32)
    block_ids = lon * lon_rows + mine * blocks + local_ids
    offset_raw = jnp.mod(own_rows(adjacent_tiles) - block_ids[:, None], total_blocks)
    offset = jnp.where(offset_raw > total_blocks // 2, offset_raw - total_blocks, offset_raw)
    window_rows = (local_ids[:, None] % size + RADIUS + offset) * half
    tapers = taper_of(offset)

    left, own, right = [], [], []
    for c in chunks:
        here, packed = packed_grams(
            mem_scalar, spread_parts[c], obs_scale, weighted, c * size
        )
        own.append(here)
        left.append(lax.ppermute(packed, ("mem", "lon"), forward))
        right.append(lax.ppermute(packed, ("mem", "lon"), backward))
    window = left + own + right

    came = []
    for c in chunks:
        blend = blends(window_rows, tapers, window[c : c + 2 * CHUNKS + 1], members, c * size, size)
        out_parts = apply_blend(mem_scalar, field_parts[c], blend)
        came.append((0, c, out_parts[0]))
        for d in far_first:
            came.append((d, c, lax.ppermute(out_parts[d], "mem", peers[d])))
    result = jnp.zeros(prior_fields.shape, BF16)
    for d, c, part in sorted(came, key=lambda item: (item[1], item[0] > 0, item[0] >= groups // 2)):
        start = ((mem ^ d) ^ flip) * blocks + c * size
        result = lax.dynamic_update_slice_in_dim(result, part, start, 1)
    return result


def solution(mesh):
    return jax.shard_map(
        on_device,
        mesh=mesh,
        in_specs=(
            P("mem", "lon", None),
            P("mem", "lon", None),
            P("lon", None),
            P("lon", None),
            P("lon"),
            P("lon", None),
        ),
        out_specs=P("mem", "lon", None),
        check_vma=False,
    )
```

```python
import functools

import jax
import jax.numpy as jnp
from jax import lax
from jax.experimental import pallas as pl
from jax.experimental.pallas import tpu as pltpu
from jax.sharding import PartitionSpec as P


RADIUS = 48
SWEEPS = 5
LANES = 128
F32 = jnp.float32
BF16 = jnp.bfloat16
VMEM_BYTES = 16 * 1024 * 1024
CROWDED_BYTES = 66_000_000
CHUNKS = 2
GROUP = 12
PAD = 1


def group_of(blocks):
    return max(u for u in range(1, GROUP + 1) if blocks % u == 0)


def vmem():
    return pl.BlockSpec(memory_space=pltpu.VMEM)


def smem():
    return pl.BlockSpec(memory_space=pltpu.SMEM)


def params(vmem_bytes=VMEM_BYTES):
    return pltpu.CompilerParams(vmem_limit_bytes=vmem_bytes)


def flip_of(groups):
    return (lax.axis_index("lon") % 2) * (groups - 1)


def pick_kernel(whole_ref, *refs, wanted, groups, size):
    outs, sems = refs[: len(wanted)], refs[len(wanted)]
    mem = lax.axis_index("mem")
    flip = flip_of(groups)
    copies = []
    for i, (d, c) in enumerate(wanted):
        start = ((mem ^ d) ^ flip) * (whole_ref.shape[1] // groups) + c * size
        rows = pl.ds(pl.multiple_of(start, 8), size)
        copies.append(pltpu.make_async_copy(whole_ref.at[:, rows, :], outs[i], sems.at[i]))
        copies[-1].start()
    for copy in copies:
        copy.wait()


def picked(x, wanted, groups, size):
    share, _, width = x.shape
    return pl.pallas_call(
        functools.partial(pick_kernel, wanted=tuple(wanted), groups=groups, size=size),
        out_shape=[jax.ShapeDtypeStruct((share, size, width), x.dtype)] * len(wanted),
        in_specs=[pl.BlockSpec(memory_space=pltpu.HBM)],
        out_specs=[vmem()] * len(wanted),
        scratch_shapes=[pltpu.SemaphoreType.DMA((len(wanted),))],
        compiler_params=params(CROWDED_BYTES),
        cost_estimate=pl.CostEstimate(
            flops=0,
            bytes_accessed=4 * share * size * width * len(wanted),
            transcendentals=0,
        ),
        name="picked",
    )(x)


def gram_kernel(*refs, groups, share, blocks, width, unroll, first):
    parts = refs[:groups]
    scale_ref, weight_ref, own_ref, send_ref, rows_ref = refs[groups:]
    members = groups * share
    half = members // 2
    tiles = width // LANES
    pitch = rows_ref.shape[1] // members
    mem = lax.axis_index("mem")
    scale = scale_ref[first : first + blocks, :]
    for d in range(groups):
        base = (mem ^ d) * (share * pitch)

        def scale_member(k, carry, part=parts[d], base=base):
            value = (part[k].astype(F32) * scale).astype(BF16).astype(F32)
            start = base + k * pitch
            for t in range(tiles):
                rows_ref[t, pl.ds(start, blocks), :] = value[:, t * LANES : (t + 1) * LANES]
            return carry

        lax.fori_loop(0, share, scale_member, 0, unroll=4)

    lane = lax.broadcasted_iota(jnp.int32, (half, LANES), 1)
    pull_lane = members + half
    from_top = (lane < members) | (lane == pull_lane) | (lane == pull_lane + 2)
    spare = LANES - pull_lane

    def block_group(i, carry):
        for u in range(unroll):
            b = i * unroll + u
            spread = jnp.concatenate(
                [rows_ref[t, pl.ds(b, members, stride=pitch), :] for t in range(tiles)], axis=1
            )
            weights = jnp.broadcast_to(weight_ref[pl.ds(first + b, 1), :], (spare, width))
            right = jnp.concatenate([spread, spread[half:], weights], axis=0).astype(BF16)
            product = lax.dot_general(
                spread.astype(BF16), right, (((1,), (1,)), ((), ())), preferred_element_type=F32
            )
            packed = jnp.where(from_top, product[:half], product[half:])
            own_ref[pl.ds(pl.multiple_of(b * half, 8), half), :] = packed
        return carry

    lax.fori_loop(0, blocks // unroll, block_group, 0)

    step = 2 * half
    lane2 = lax.broadcasted_iota(jnp.int32, (step, LANES), 1)

    def finish(i, carry):
        at = pl.ds(pl.multiple_of(i * step, 16), step)
        value = own_ref[at, :]
        low = value - value.astype(BF16).astype(F32)
        is_low = lane2 >= pull_lane + 2
        send_ref[at, :] = jnp.where(is_low, low, value).astype(BF16)
        own_ref[at, :] = jnp.where(is_low, 0.0, value)
        return carry

    lax.fori_loop(0, blocks // 2, finish, 0, unroll=2)


def packed_grams(parts, scale, weighted, first):
    groups = len(parts)
    share, blocks, width = parts[0].shape
    members = groups * share
    half = members // 2
    assert members + half + 4 <= LANES and half % 8 == 0
    flat = (blocks * half, LANES)
    return pl.pallas_call(
        functools.partial(
            gram_kernel,
            groups=groups,
            share=share,
            blocks=blocks,
            width=width,
            unroll=group_of(blocks),
            first=first,
        ),
        out_shape=(jax.ShapeDtypeStruct(flat, F32), jax.ShapeDtypeStruct(flat, BF16)),
        in_specs=[vmem()] * (groups + 2),
        out_specs=(vmem(), vmem()),
        scratch_shapes=[pltpu.VMEM((width // LANES, members * (blocks + PAD), LANES), F32)],
        compiler_params=params(),
        cost_estimate=pl.CostEstimate(
            flops=2 * blocks * members * width * LANES,
            bytes_accessed=members * blocks * width * 2,
            transcendentals=0,
        ),
        name="packed_grams",
    )(*parts, scale, weighted)


def blend_kernel(
    row_ref, taper_ref, *refs, members, neighbours, blocks, unroll, first
):
    *pieces, blend_ref, window_ref = refs
    half = members // 2
    pull_lane = members + half
    filled = 0
    for piece in pieces:
        window_ref[pl.ds(filled, piece.shape[0]), :] = piece[...].astype(F32)
        filled += piece.shape[0]
    full = (members, LANES)
    lane = lax.broadcasted_iota(jnp.int32, full, 1)
    row = lax.broadcasted_iota(jnp.int32, full, 0)
    eye = (lane == row).astype(F32)
    in_matrix = lax.broadcasted_iota(jnp.int32, (1, LANES), 1) < members
    share_row = jnp.where(in_matrix, 1.0 / (members - 1), 0.0)
    left_half = lax.broadcasted_iota(jnp.int32, (half, LANES), 1) < half
    pad_rows = jnp.zeros((LANES - half, LANES), F32)
    pad_depth = jnp.zeros((LANES - members, LANES), BF16)

    def total(x):
        return jnp.sum(jnp.sum(x, axis=0, keepdims=True), axis=1, keepdims=True)

    def times(lhs, rhs):
        return jnp.dot(
            lhs, jnp.concatenate([rhs, pad_depth], axis=0), preferred_element_type=F32
        )

    def localized_sum(b):
        packed = None
        for n in range(neighbours):
            start = pl.multiple_of(row_ref[first + b, n], 8)
            term = taper_ref[first + b, n] * window_ref[pl.ds(start, half), :]
            packed = term if packed is None else packed + term
        turned = jnp.concatenate([packed, pad_rows], axis=0).T
        low_rows = jnp.where(
            left_half, turned[half:members], pltpu.roll(packed, LANES - half, axis=1)
        )
        pull = turned[pull_lane : pull_lane + 8]
        pull_row = (pull[0:1] + pull[2:3]) + pltpu.roll(pull[1:2] + pull[3:4], half, axis=1)
        return jnp.concatenate([packed, low_rows], axis=0) * share_row, pull_row

    def block_group(i, carry):
        group = range(unroll)
        ids = [i * unroll + u for u in group]
        sums = [localized_sum(b) for b in ids]
        gram = [g for g, _ in sums]
        trace = [total(g * eye) for g in gram]
        square = [total(g * g) for g in gram]
        frob2 = [square[u] + 2.0 * trace[u] + float(members) for u in group]
        inv = [lax.rsqrt(f) for f in frob2]
        mean = [t * (1.0 / members) for t in trace]
        y = [(1.0 + mean[u]) * inv[u] for u in group]
        y_rest = [(gram[u] - mean[u] * eye) * inv[u] for u in group]
        p = [-0.5 * v for v in y]
        p_rest = [-0.5 * v for v in y_rest]
        s = [1.5 + v for v in p]
        y_low = [v.astype(BF16) for v in y_rest]
        p_low = [v.astype(BF16) for v in p_rest]
        prod = [times(y_low[u], p_low[u]) for u in group]
        z = [-0.5 * v for v in s]
        z_rest = [-0.5 * v for v in p_rest]
        y_rest = [(s[u] * y_rest[u] + y[u] * p_rest[u]) + prod[u] for u in group]
        y = [s[u] * y[u] for u in group]
        for sweep in range(1, SWEEPS):
            last = sweep == SWEEPS - 1
            y_low = [v.astype(BF16) for v in y_rest]
            z_low = [v.astype(BF16) for v in z_rest]
            prod = [times(z_low[u], y_low[u]) for u in group]
            p = [z[u] * y[u] for u in group]
            p_rest = [(z[u] * y_rest[u] + y[u] * z_rest[u]) + prod[u] for u in group]
            s = [1.5 + v for v in p]
            p_low = [v.astype(BF16) for v in p_rest]
            if last:
                prod = [times(z_low[u], p_low[u]) for u in group]
                z_rest = [(s[u] * z_rest[u] + z[u] * p_rest[u]) + prod[u] for u in group]
            else:
                prod = [
                    times(jnp.concatenate([y_low[u], z_low[u]], axis=0), p_low[u])
                    for u in group
                ]
                y_rest = [
                    (s[u] * y_rest[u] + y[u] * p_rest[u]) + prod[u][:members] for u in group
                ]
                z_rest = [
                    (s[u] * z_rest[u] + z[u] * p_rest[u]) + prod[u][members:] for u in group
                ]
                y = [s[u] * y[u] for u in group]
            z = [s[u] * z[u] for u in group]
        root = [z[u] * eye + z_rest[u] for u in group]
        norm = [-2.0 * jnp.sqrt(v) for v in inv]
        inner = [
            jnp.sum(root[u] * sums[u][1], axis=1, keepdims=True) for u in group
        ]
        shift = [
            jnp.sum(root[u] * inner[u], axis=0, keepdims=True)
            * (norm[u] * norm[u] * (1.0 / (members - 1)))
            for u in group
        ]
        for u in group:
            at = pl.ds(pl.multiple_of(ids[u] * members, 16), members)
            blend_ref[at, :] = (norm[u] * root[u] + shift[u]).astype(BF16)
        return carry

    lax.fori_loop(0, blocks // unroll, block_group, 0)


def blends(rows, tapers, window, members, first, blocks):
    neighbours = rows.shape[1]
    window_rows = sum(piece.shape[0] for piece in window)
    return pl.pallas_call(
        functools.partial(
            blend_kernel,
            members=members,
            neighbours=neighbours,
            blocks=blocks,
            unroll=group_of(blocks),
            first=first,
        ),
        out_shape=jax.ShapeDtypeStruct((blocks * members, LANES), BF16),
        in_specs=[smem(), smem()] + [vmem()] * len(window),
        out_specs=vmem(),
        scratch_shapes=[pltpu.VMEM((window_rows, LANES), F32)],
        compiler_params=params(),
        cost_estimate=pl.CostEstimate(
            flops=blocks * 24 * members * members * LANES,
            bytes_accessed=3 * window_rows * LANES,
            transcendentals=0,
        ),
        name="blends",
    )(rows, tapers, *window)


def apply_kernel(*refs, groups, share, blocks, width, unroll):
    parts = refs[:groups]
    blend_ref = refs[groups]
    outs = refs[groups + 1 : 2 * groups + 1]
    center_ref, rows_ref = refs[2 * groups + 1 :]
    members = groups * share
    tiles = width // LANES
    pitch = rows_ref.shape[1] // members
    mem = lax.axis_index("mem")
    zero = jnp.zeros((blocks, width), F32)
    center = zero
    for d in range(groups):
        center = lax.fori_loop(
            0, share, lambda k, acc, part=parts[d]: acc + part[k].astype(F32), center, unroll=4
        )
    center = center * (1.0 / members)
    center_ref[...] = center
    for d in range(groups):
        base = (mem ^ d) * (share * pitch)

        def perturb(k, carry, part=parts[d], base=base):
            value = (part[k].astype(F32) - center_ref[...]).astype(BF16).astype(F32)
            start = base + k * pitch
            for t in range(tiles):
                rows_ref[t, pl.ds(start, blocks), :] = value[:, t * LANES : (t + 1) * LANES]
            return carry

        lax.fori_loop(0, share, perturb, 0, unroll=4)

    pad_depth = jnp.zeros((LANES - members, width), BF16)

    def block_group(i, carry):
        for u in range(unroll):
            b = i * unroll + u
            at = pl.ds(b, members, stride=pitch)
            anomalies = jnp.concatenate([rows_ref[t, at, :] for t in range(tiles)], axis=1)
            mixed = jnp.dot(
                blend_ref[pl.ds(pl.multiple_of(b * members, 16), members), :],
                jnp.concatenate([anomalies.astype(BF16), pad_depth], axis=0),
                preferred_element_type=F32,
            )
            for t in range(tiles):
                rows_ref[t, at, :] = mixed[:, t * LANES : (t + 1) * LANES]
        return carry

    lax.fori_loop(0, blocks // unroll, block_group, 0)

    for d in range(groups):
        base = (mem ^ d) * (share * pitch)

        def finish(k, carry, out=outs[d], base=base):
            start = base + k * pitch
            mixed = jnp.concatenate(
                [rows_ref[t, pl.ds(start, blocks), :] for t in range(tiles)], axis=1
            )
            out[k] = (center_ref[...] + mixed).astype(BF16)
            return carry

        lax.fori_loop(0, share, finish, 0, unroll=4)


def apply_blend(parts, blend):
    groups = len(parts)
    share, blocks, width = parts[0].shape
    members = groups * share
    part = jax.ShapeDtypeStruct((share, blocks, width), BF16)
    return pl.pallas_call(
        functools.partial(
            apply_kernel, groups=groups, share=share, blocks=blocks, width=width, unroll=group_of(blocks)
        ),
        out_shape=(part,) * groups,
        in_specs=[vmem()] * (groups + 1),
        out_specs=(vmem(),) * groups,
        scratch_shapes=[
            pltpu.VMEM((blocks, width), F32),
            pltpu.VMEM((width // LANES, members * (blocks + PAD), LANES), F32),
        ],
        compiler_params=params(),
        cost_estimate=pl.CostEstimate(
            flops=2 * blocks * members * LANES * width,
            bytes_accessed=2 * members * blocks * width * 2,
            transcendentals=0,
        ),
        name="apply_blend",
    )(*parts, blend)


def taper_of(offset):
    ratio = offset.astype(F32) / RADIUS
    return 1.0 / (1.0 + ratio * ratio)


def on_device(
    prior_fields,
    scaled_sensor_spread,
    measured_misfit,
    inverse_error_variance,
    active_sensor_number,
    adjacent_tiles,
):
    groups = lax.axis_size("mem")
    belts = lax.axis_size("lon")
    share, lon_rows, width = scaled_sensor_spread.shape
    members = groups * share
    half = members // 2
    total_blocks = lon_rows * belts
    blocks = lon_rows // groups
    assert groups & (groups - 1) == 0 and blocks == RADIUS
    mem = lax.axis_index("mem")
    lon = lax.axis_index("lon")
    flip = flip_of(groups)
    mine = mem ^ flip
    peers = [[(i, i ^ d) for i in range(groups)] for d in range(groups)]
    far_first = sorted(range(1, groups), key=lambda d: (d < groups // 2, d))

    def holder(g):
        belt, q = divmod(g % (belts * groups), groups)
        return (q ^ ((belt % 2) * (groups - 1))) * belts + belt

    ring = range(belts * groups)
    forward = [(holder(g), holder(g + 1)) for g in ring]
    backward = [(holder(g), holder(g - 1)) for g in ring]

    size = blocks // CHUNKS
    chunks = range(CHUNKS)
    last = None

    def pieces(x, wanted):
        nonlocal last
        taken = {}
        for d, c in wanted:
            if last is not None:
                x, _ = lax.optimization_barrier((x, last))
            start = ((mem ^ d) ^ flip) * blocks + c * size
            last = taken[d, c] = lax.dynamic_slice_in_dim(x, start, size, 1)
        return taken

    def own_rows(x):
        return lax.dynamic_slice_in_dim(x, mine * blocks, blocks, 0)

    def exchanged(taken, c):
        parts = {d: lax.ppermute(taken[d, c], "mem", peers[d]) for d in far_first}
        parts[0] = taken[0, c]
        return [parts[d] for d in range(groups)]

    order = far_first + [0]
    everything = [(d, c) for c in chunks for d in order]
    (last,) = picked(scaled_sensor_spread, everything[:1], groups, size)
    spread_taken = {everything[0]: last} | pieces(scaled_sensor_spread, everything[1:])
    field_taken = pieces(prior_fields, everything)
    spread_parts = [exchanged(spread_taken, c) for c in chunks]
    field_parts = [exchanged(field_taken, c) for c in chunks]

    slot_ids = jnp.arange(width, dtype=jnp.int32)
    live = (slot_ids[None, :] < own_rows(active_sensor_number)[:, None]).astype(F32)
    obs_scale = jnp.sqrt(own_rows(inverse_error_variance) * live)
    weighted = own_rows(measured_misfit) * obs_scale
    local_ids = jnp.arange(blocks, dtype=jnp.int32)
    block_ids = lon * lon_rows + mine * blocks + local_ids
    offset_raw = jnp.mod(own_rows(adjacent_tiles) - block_ids[:, None], total_blocks)
    offset = jnp.where(offset_raw > total_blocks // 2, offset_raw - total_blocks, offset_raw)
    window_rows = (local_ids[:, None] % size + RADIUS + offset) * half
    tapers = taper_of(offset)

    left, own, right = [], [], []
    for c in chunks:
        here, packed = packed_grams(
            spread_parts[c], obs_scale, weighted, c * size
        )
        own.append(here)
        left.append(lax.ppermute(packed, ("mem", "lon"), forward))
        right.append(lax.ppermute(packed, ("mem", "lon"), backward))
    window = left + own + right

    came = []
    for c in chunks:
        blend = blends(window_rows, tapers, window[c : c + 2 * CHUNKS + 1], members, c * size, size)
        out_parts = apply_blend(field_parts[c], blend)
        came.append((0, c, out_parts[0]))
        for d in far_first:
            came.append((d, c, lax.ppermute(out_parts[d], "mem", peers[d])))
    result = jnp.zeros(prior_fields.shape, BF16)
    for d, c, part in sorted(came, key=lambda item: (item[1], item[0] > 0, item[0] >= groups // 2)):
        start = ((mem ^ d) ^ flip) * blocks + c * size
        result = lax.dynamic_update_slice_in_dim(result, part, start, 1)
    return result


def solution(mesh):
    return jax.shard_map(
        on_device,
        mesh=mesh,
        in_specs=(
            P("mem", "lon", None),
            P("mem", "lon", None),
            P("lon", None),
            P("lon", None),
            P("lon"),
            P("lon", None),
        ),
        out_specs=P("mem", "lon", None),
        check_vma=False,
    )
```

```python
import functools

import jax
import jax.numpy as jnp
from jax import lax
from jax.experimental import pallas as pl
from jax.experimental.pallas import tpu as pltpu
from jax.sharding import PartitionSpec as P


RADIUS = 48
SWEEPS = 5
LANES = 128
F32 = jnp.float32
BF16 = jnp.bfloat16
VMEM_BYTES = 16 * 1024 * 1024
CROWDED_BYTES = 66_000_000
CHUNKS = 2
GROUP = 12
PAD = 1


def group_of(blocks):
    return max(u for u in range(1, GROUP + 1) if blocks % u == 0)


def vmem():
    return pl.BlockSpec(memory_space=pltpu.VMEM)


def smem():
    return pl.BlockSpec(memory_space=pltpu.SMEM)


def params(vmem_bytes=VMEM_BYTES):
    return pltpu.CompilerParams(vmem_limit_bytes=vmem_bytes)


def flip_of(groups):
    return (lax.axis_index("lon") % 2) * (groups - 1)


def pick_kernel(whole_ref, *refs, wanted, groups, size):
    outs, sems = refs[: len(wanted)], refs[len(wanted)]
    mem = lax.axis_index("mem")
    flip = flip_of(groups)
    copies = []
    for i, (d, c) in enumerate(wanted):
        start = ((mem ^ d) ^ flip) * (whole_ref.shape[1] // groups) + c * size
        rows = pl.ds(pl.multiple_of(start, 8), size)
        copies.append(pltpu.make_async_copy(whole_ref.at[:, rows, :], outs[i], sems.at[i]))
        copies[-1].start()
    for copy in copies:
        copy.wait()


def picked(x, wanted, groups, size):
    share, _, width = x.shape
    return pl.pallas_call(
        functools.partial(pick_kernel, wanted=tuple(wanted), groups=groups, size=size),
        out_shape=[jax.ShapeDtypeStruct((share, size, width), x.dtype)] * len(wanted),
        in_specs=[pl.BlockSpec(memory_space=pltpu.HBM)],
        out_specs=[vmem()] * len(wanted),
        scratch_shapes=[pltpu.SemaphoreType.DMA((len(wanted),))],
        compiler_params=params(CROWDED_BYTES),
        cost_estimate=pl.CostEstimate(
            flops=0,
            bytes_accessed=4 * share * size * width * len(wanted),
            transcendentals=0,
        ),
        name="picked",
    )(x)


FOLD = 8


def used_lanes(members):
    return members + 5


def low_lanes(members):
    rows = members // 2 - FOLD
    lane = lax.broadcasted_iota(jnp.int32, (rows, LANES), 1)
    row = lax.broadcasted_iota(jnp.int32, (rows, LANES), 0)
    first = used_lanes(members) - 2
    turn = used_lanes(members) - (LANES - used_lanes(members))
    folded = (row >= FOLD) & (row < 2 * FOLD) & (lane >= first + turn)
    return ((lane >= first) & (lane < first + 2)) | (folded & (lane < first + 2 + turn))


def gram_kernel(*refs, groups, share, blocks, width, unroll, first):
    parts = refs[:groups]
    scale_ref, weight_ref, own_ref, send_ref, rows_ref = refs[groups:]
    members = groups * share
    half = members // 2
    tiles = width // LANES
    pitch = rows_ref.shape[1] // members
    mem = lax.axis_index("mem")
    scale = scale_ref[first : first + blocks, :]
    for d in range(groups):
        base = (mem ^ d) * (share * pitch)

        def scale_member(k, carry, part=parts[d], base=base):
            value = (part[k].astype(F32) * scale).astype(BF16).astype(F32)
            start = base + k * pitch
            for t in range(tiles):
                rows_ref[t, pl.ds(start, blocks), :] = value[:, t * LANES : (t + 1) * LANES]
            return carry

        lax.fori_loop(0, share, scale_member, 0, unroll=4)

    used = used_lanes(members)
    spare = LANES - used
    packed_rows = half - FOLD
    lane = lax.broadcasted_iota(jnp.int32, (half, LANES), 1)
    row = lax.broadcasted_iota(jnp.int32, (half, LANES), 0)
    upper = (lane < half) & (lane > row)
    c_diagonal = lane == row + half
    from_bottom = (lane == members + 2) | (lane == members + 4)
    in_use = lax.broadcasted_iota(jnp.int32, (FOLD, LANES), 1) < used

    def block_group(i, carry):
        for u in range(unroll):
            b = i * unroll + u
            spread = jnp.concatenate(
                [rows_ref[t, pl.ds(b, members, stride=pitch), :] for t in range(tiles)], axis=1
            )
            weights = jnp.broadcast_to(weight_ref[pl.ds(first + b, 1), :], (8, width))
            filler = jnp.zeros((LANES - members - 8, width), F32)
            right = jnp.concatenate([spread, weights, filler], axis=0).astype(BF16)
            product = lax.dot_general(
                spread.astype(BF16), right, (((1,), (1,)), ((), ())), preferred_element_type=F32
            )
            top, bottom = product[:half], product[half:]
            diagonal = jnp.sum(jnp.where(c_diagonal, bottom, 0.0), axis=1, keepdims=True)
            packed = jnp.where(upper, pltpu.roll(bottom, LANES - half, axis=1), top)
            packed = jnp.where(from_bottom, bottom, packed)
            packed = jnp.where(lane == members, diagonal, packed)
            tail = packed[packed_rows:]
            own_ref[pl.ds(pl.multiple_of(b * packed_rows, 8), packed_rows), :] = jnp.concatenate(
                [
                    jnp.where(in_use, packed[:FOLD], pltpu.roll(tail, used, axis=1)),
                    jnp.where(
                        in_use, packed[FOLD : 2 * FOLD], pltpu.roll(tail, used - spare, axis=1)
                    ),
                    packed[2 * FOLD : packed_rows],
                ],
                axis=0,
            )
        return carry

    lax.fori_loop(0, blocks // unroll, block_group, 0)
    is_low = low_lanes(members)

    def finish(i, carry):
        at = pl.ds(pl.multiple_of(i * packed_rows, 16), packed_rows)
        value = own_ref[at, :]
        low = value - value.astype(BF16).astype(F32)
        send_ref[at, :] = jnp.where(is_low, low, value).astype(BF16)
        own_ref[at, :] = jnp.where(is_low, 0.0, value)
        return carry

    lax.fori_loop(0, blocks, finish, 0, unroll=4)


def packed_grams(parts, scale, weighted, first):
    groups = len(parts)
    share, blocks, width = parts[0].shape
    members = groups * share
    half = members // 2
    spare = LANES - used_lanes(members)
    assert half % 8 == 0 and (half - FOLD) % 16 == 0 and half >= 3 * FOLD
    assert spare >= used_lanes(members) - spare and members + 8 <= LANES
    flat = (blocks * (half - FOLD), LANES)
    return pl.pallas_call(
        functools.partial(
            gram_kernel,
            groups=groups,
            share=share,
            blocks=blocks,
            width=width,
            unroll=group_of(blocks),
            first=first,
        ),
        out_shape=(jax.ShapeDtypeStruct(flat, F32), jax.ShapeDtypeStruct(flat, BF16)),
        in_specs=[vmem()] * (groups + 2),
        out_specs=(vmem(), vmem()),
        scratch_shapes=[pltpu.VMEM((width // LANES, members * (blocks + PAD), LANES), F32)],
        compiler_params=params(),
        cost_estimate=pl.CostEstimate(
            flops=2 * blocks * members * width * LANES,
            bytes_accessed=members * blocks * width * 2,
            transcendentals=0,
        ),
        name="packed_grams",
    )(*parts, scale, weighted)


def blend_kernel(
    row_ref, taper_ref, *refs, members, neighbours, blocks, unroll, first
):
    *pieces, blend_ref, window_ref = refs
    half = members // 2
    used = used_lanes(members)
    spare = LANES - used
    packed_rows = half - FOLD
    filled = 0
    for piece in pieces:
        window_ref[pl.ds(filled, piece.shape[0]), :] = piece[...].astype(F32)
        filled += piece.shape[0]
    full = (members, LANES)
    lane = lax.broadcasted_iota(jnp.int32, full, 1)
    row = lax.broadcasted_iota(jnp.int32, full, 0)
    eye = (lane == row).astype(F32)
    in_matrix = lax.broadcasted_iota(jnp.int32, (1, LANES), 1) < members
    share_row = jnp.where(in_matrix, 1.0 / (members - 1), 0.0)
    half_lane = lax.broadcasted_iota(jnp.int32, (half, LANES), 1)
    half_row = lax.broadcasted_iota(jnp.int32, (half, LANES), 0)
    in_first = lax.broadcasted_iota(jnp.int32, (FOLD, LANES), 1) < spare
    pad_rows = jnp.zeros((LANES - half, LANES), F32)
    pad_depth = jnp.zeros((LANES - members, LANES), BF16)

    def total(x):
        return jnp.sum(jnp.sum(x, axis=0, keepdims=True), axis=1, keepdims=True)

    def times(lhs, rhs):
        return jnp.dot(
            lhs, jnp.concatenate([rhs, pad_depth], axis=0), preferred_element_type=F32
        )

    def localized_sum(b):
        packed = None
        for n in range(neighbours):
            start = pl.multiple_of(row_ref[first + b, n], 8)
            term = taper_ref[first + b, n] * window_ref[pl.ds(start, packed_rows), :]
            packed = term if packed is None else packed + term
        tail = jnp.where(
            in_first,
            pltpu.roll(packed[:FOLD], LANES - used, axis=1),
            pltpu.roll(packed[FOLD : 2 * FOLD], LANES - (used - spare), axis=1),
        )
        packed = jnp.concatenate([packed, tail], axis=0)
        turned = jnp.concatenate([packed, pad_rows], axis=0).T
        extra = turned[members : members + 8]
        lower = turned[:half]
        c_part = jnp.where(half_lane > half_row, packed, lower)
        c_part = jnp.where(half_lane == half_row, extra[0:1], c_part)
        top = jnp.where((half_lane > half_row) & (half_lane < half), lower, packed)
        bottom = jnp.where(half_lane < half, turned[half:members], pltpu.roll(c_part, half, axis=1))
        pull_row = (extra[1:2] + extra[3:4]) + pltpu.roll(extra[2:3] + extra[4:5], half, axis=1)
        return jnp.concatenate([top, bottom], axis=0) * share_row, pull_row

    def block_group(i, carry):
        group = range(unroll)
        ids = [i * unroll + u for u in group]
        sums = [localized_sum(b) for b in ids]
        gram = [g for g, _ in sums]
        trace = [total(g * eye) for g in gram]
        square = [total(g * g) for g in gram]
        frob2 = [square[u] + 2.0 * trace[u] + float(members) for u in group]
        inv = [lax.rsqrt(f) for f in frob2]
        mean = [t * (1.0 / members) for t in trace]
        y = [(1.0 + mean[u]) * inv[u] for u in group]
        y_rest = [(gram[u] - mean[u] * eye) * inv[u] for u in group]
        p = [-0.5 * v for v in y]
        p_rest = [-0.5 * v for v in y_rest]
        s = [1.5 + v for v in p]
        y_low = [v.astype(BF16) for v in y_rest]
        p_low = [v.astype(BF16) for v in p_rest]
        prod = [times(y_low[u], p_low[u]) for u in group]
        z = [-0.5 * v for v in s]
        z_rest = [-0.5 * v for v in p_rest]
        y_rest = [(s[u] * y_rest[u] + y[u] * p_rest[u]) + prod[u] for u in group]
        y = [s[u] * y[u] for u in group]
        for sweep in range(1, SWEEPS):
            last = sweep == SWEEPS - 1
            y_low = [v.astype(BF16) for v in y_rest]
            z_low = [v.astype(BF16) for v in z_rest]
            prod = [times(z_low[u], y_low[u]) for u in group]
            p = [z[u] * y[u] for u in group]
            p_rest = [(z[u] * y_rest[u] + y[u] * z_rest[u]) + prod[u] for u in group]
            s = [1.5 + v for v in p]
            p_low = [v.astype(BF16) for v in p_rest]
            if last:
                prod = [times(z_low[u], p_low[u]) for u in group]
                z_rest = [(s[u] * z_rest[u] + z[u] * p_rest[u]) + prod[u] for u in group]
            else:
                prod = [
                    times(jnp.concatenate([y_low[u], z_low[u]], axis=0), p_low[u])
                    for u in group
                ]
                y_rest = [
                    (s[u] * y_rest[u] + y[u] * p_rest[u]) + prod[u][:members] for u in group
                ]
                z_rest = [
                    (s[u] * z_rest[u] + z[u] * p_rest[u]) + prod[u][members:] for u in group
                ]
                y = [s[u] * y[u] for u in group]
            z = [s[u] * z[u] for u in group]
        root = [z[u] * eye + z_rest[u] for u in group]
        norm = [-2.0 * jnp.sqrt(v) for v in inv]
        inner = [
            jnp.sum(root[u] * sums[u][1], axis=1, keepdims=True) for u in group
        ]
        shift = [
            jnp.sum(root[u] * inner[u], axis=0, keepdims=True)
            * (norm[u] * norm[u] * (1.0 / (members - 1)))
            for u in group
        ]
        for u in group:
            at = pl.ds(pl.multiple_of(ids[u] * members, 16), members)
            blend_ref[at, :] = (norm[u] * root[u] + shift[u]).astype(BF16)
        return carry

    lax.fori_loop(0, blocks // unroll, block_group, 0)


def blends(rows, tapers, window, members, first, blocks):
    neighbours = rows.shape[1]
    window_rows = sum(piece.shape[0] for piece in window)
    return pl.pallas_call(
        functools.partial(
            blend_kernel,
            members=members,
            neighbours=neighbours,
            blocks=blocks,
            unroll=group_of(blocks),
            first=first,
        ),
        out_shape=jax.ShapeDtypeStruct((blocks * members, LANES), BF16),
        in_specs=[smem(), smem()] + [vmem()] * len(window),
        out_specs=vmem(),
        scratch_shapes=[pltpu.VMEM((window_rows, LANES), F32)],
        compiler_params=params(),
        cost_estimate=pl.CostEstimate(
            flops=blocks * 24 * members * members * LANES,
            bytes_accessed=3 * window_rows * LANES,
            transcendentals=0,
        ),
        name="blends",
    )(rows, tapers, *window)


def apply_kernel(*refs, groups, share, blocks, width, unroll):
    parts = refs[:groups]
    blend_ref = refs[groups]
    outs = refs[groups + 1 : 2 * groups + 1]
    center_ref, rows_ref = refs[2 * groups + 1 :]
    members = groups * share
    tiles = width // LANES
    pitch = rows_ref.shape[1] // members
    mem = lax.axis_index("mem")
    zero = jnp.zeros((blocks, width), F32)
    center = zero
    for d in range(groups):
        center = lax.fori_loop(
            0, share, lambda k, acc, part=parts[d]: acc + part[k].astype(F32), center, unroll=4
        )
    center = center * (1.0 / members)
    center_ref[...] = center
    for d in range(groups):
        base = (mem ^ d) * (share * pitch)

        def perturb(k, carry, part=parts[d], base=base):
            value = (part[k].astype(F32) - center_ref[...]).astype(BF16).astype(F32)
            start = base + k * pitch
            for t in range(tiles):
                rows_ref[t, pl.ds(start, blocks), :] = value[:, t * LANES : (t + 1) * LANES]
            return carry

        lax.fori_loop(0, share, perturb, 0, unroll=4)

    pad_depth = jnp.zeros((LANES - members, width), BF16)

    def block_group(i, carry):
        for u in range(unroll):
            b = i * unroll + u
            at = pl.ds(b, members, stride=pitch)
            anomalies = jnp.concatenate([rows_ref[t, at, :] for t in range(tiles)], axis=1)
            mixed = jnp.dot(
                blend_ref[pl.ds(pl.multiple_of(b * members, 16), members), :],
                jnp.concatenate([anomalies.astype(BF16), pad_depth], axis=0),
                preferred_element_type=F32,
            )
            for t in range(tiles):
                rows_ref[t, at, :] = mixed[:, t * LANES : (t + 1) * LANES]
        return carry

    lax.fori_loop(0, blocks // unroll, block_group, 0)

    for d in range(groups):
        base = (mem ^ d) * (share * pitch)

        def finish(k, carry, out=outs[d], base=base):
            start = base + k * pitch
            mixed = jnp.concatenate(
                [rows_ref[t, pl.ds(start, blocks), :] for t in range(tiles)], axis=1
            )
            out[k] = (center_ref[...] + mixed).astype(BF16)
            return carry

        lax.fori_loop(0, share, finish, 0, unroll=4)


def apply_blend(parts, blend):
    groups = len(parts)
    share, blocks, width = parts[0].shape
    members = groups * share
    part = jax.ShapeDtypeStruct((share, blocks, width), BF16)
    return pl.pallas_call(
        functools.partial(
            apply_kernel, groups=groups, share=share, blocks=blocks, width=width, unroll=group_of(blocks)
        ),
        out_shape=(part,) * groups,
        in_specs=[vmem()] * (groups + 1),
        out_specs=(vmem(),) * groups,
        scratch_shapes=[
            pltpu.VMEM((blocks, width), F32),
            pltpu.VMEM((width // LANES, members * (blocks + PAD), LANES), F32),
        ],
        compiler_params=params(),
        cost_estimate=pl.CostEstimate(
            flops=2 * blocks * members * LANES * width,
            bytes_accessed=2 * members * blocks * width * 2,
            transcendentals=0,
        ),
        name="apply_blend",
    )(*parts, blend)


def taper_of(offset):
    ratio = offset.astype(F32) / RADIUS
    return 1.0 / (1.0 + ratio * ratio)


def on_device(
    prior_fields,
    scaled_sensor_spread,
    measured_misfit,
    inverse_error_variance,
    active_sensor_number,
    adjacent_tiles,
):
    groups = lax.axis_size("mem")
    belts = lax.axis_size("lon")
    share, lon_rows, width = scaled_sensor_spread.shape
    members = groups * share
    half = members // 2
    total_blocks = lon_rows * belts
    blocks = lon_rows // groups
    assert groups & (groups - 1) == 0 and blocks == RADIUS
    mem = lax.axis_index("mem")
    lon = lax.axis_index("lon")
    flip = flip_of(groups)
    mine = mem ^ flip
    peers = [[(i, i ^ d) for i in range(groups)] for d in range(groups)]
    far_first = sorted(range(1, groups), key=lambda d: (d < groups // 2, d))

    def holder(g):
        belt, q = divmod(g % (belts * groups), groups)
        return (q ^ ((belt % 2) * (groups - 1))) * belts + belt

    ring = range(belts * groups)
    forward = [(holder(g), holder(g + 1)) for g in ring]
    backward = [(holder(g), holder(g - 1)) for g in ring]

    size = blocks // CHUNKS
    chunks = range(CHUNKS)
    last = None

    def pieces(x, wanted):
        nonlocal last
        taken = {}
        for d, c in wanted:
            if last is not None:
                x, _ = lax.optimization_barrier((x, last))
            start = ((mem ^ d) ^ flip) * blocks + c * size
            last = taken[d, c] = lax.dynamic_slice_in_dim(x, start, size, 1)
        return taken

    def own_rows(x):
        return lax.dynamic_slice_in_dim(x, mine * blocks, blocks, 0)

    def exchanged(taken, c):
        parts = {d: lax.ppermute(taken[d, c], "mem", peers[d]) for d in far_first}
        parts[0] = taken[0, c]
        return [parts[d] for d in range(groups)]

    order = far_first + [0]
    everything = [(d, c) for c in chunks for d in order]
    (last,) = picked(scaled_sensor_spread, everything[:1], groups, size)
    spread_taken = {everything[0]: last} | pieces(scaled_sensor_spread, everything[1:])
    field_taken = pieces(prior_fields, everything)
    spread_parts = [exchanged(spread_taken, c) for c in chunks]
    field_parts = [exchanged(field_taken, c) for c in chunks]

    slot_ids = jnp.arange(width, dtype=jnp.int32)
    live = (slot_ids[None, :] < own_rows(active_sensor_number)[:, None]).astype(F32)
    obs_scale = jnp.sqrt(own_rows(inverse_error_variance) * live)
    weighted = own_rows(measured_misfit) * obs_scale
    local_ids = jnp.arange(blocks, dtype=jnp.int32)
    block_ids = lon * lon_rows + mine * blocks + local_ids
    offset_raw = jnp.mod(own_rows(adjacent_tiles) - block_ids[:, None], total_blocks)
    offset = jnp.where(offset_raw > total_blocks // 2, offset_raw - total_blocks, offset_raw)
    window_rows = (local_ids[:, None] % size + RADIUS + offset) * (half - FOLD)
    tapers = taper_of(offset)

    left, own, right = [], [], []
    for c in chunks:
        here, packed = packed_grams(
            spread_parts[c], obs_scale, weighted, c * size
        )
        own.append(here)
        left.append(lax.ppermute(packed, ("mem", "lon"), forward))
        right.append(lax.ppermute(packed, ("mem", "lon"), backward))
    window = left + own + right

    came = []
    for c in chunks:
        blend = blends(window_rows, tapers, window[c : c + 2 * CHUNKS + 1], members, c * size, size)
        out_parts = apply_blend(field_parts[c], blend)
        came.append((0, c, out_parts[0]))
        for d in far_first:
            came.append((d, c, lax.ppermute(out_parts[d], "mem", peers[d])))
    result = jnp.zeros(prior_fields.shape, BF16)
    for d, c, part in sorted(came, key=lambda item: (item[1], item[0] > 0, item[0] >= groups // 2)):
        start = ((mem ^ d) ^ flip) * blocks + c * size
        result = lax.dynamic_update_slice_in_dim(result, part, start, 1)
    return result


def solution(mesh):
    return jax.shard_map(
        on_device,
        mesh=mesh,
        in_specs=(
            P("mem", "lon", None),
            P("mem", "lon", None),
            P("lon", None),
            P("lon", None),
            P("lon"),
            P("lon", None),
        ),
        out_specs=P("mem", "lon", None),
        check_vma=False,
    )
```

```python
import functools

import jax
import jax.numpy as jnp
from jax import lax
from jax.experimental import pallas as pl
from jax.experimental.pallas import tpu as pltpu
from jax.sharding import PartitionSpec as P


RADIUS = 48
SWEEPS = 5
LANES = 128
F32 = jnp.float32
BF16 = jnp.bfloat16
VMEM_BYTES = 16 * 1024 * 1024
CROWDED_BYTES = 66_000_000
CHUNKS = 2
GROUP = 12
PAD = 1


def group_of(blocks):
    return max(u for u in range(1, GROUP + 1) if blocks % u == 0)


def vmem():
    return pl.BlockSpec(memory_space=pltpu.VMEM)


def smem():
    return pl.BlockSpec(memory_space=pltpu.SMEM)


def params(vmem_bytes=VMEM_BYTES):
    return pltpu.CompilerParams(vmem_limit_bytes=vmem_bytes)


def flip_of(groups):
    return (lax.axis_index("lon") % 2) * (groups - 1)


def pick_kernel(whole_ref, *refs, wanted, groups, size):
    outs, sems = refs[: len(wanted)], refs[len(wanted)]
    mem = lax.axis_index("mem")
    flip = flip_of(groups)
    copies = []
    for i, (d, c) in enumerate(wanted):
        start = ((mem ^ d) ^ flip) * (whole_ref.shape[1] // groups) + c * size
        rows = pl.ds(pl.multiple_of(start, 8), size)
        copies.append(pltpu.make_async_copy(whole_ref.at[:, rows, :], outs[i], sems.at[i]))
        copies[-1].start()
    for copy in copies:
        copy.wait()


def picked(x, wanted, groups, size):
    share, _, width = x.shape
    return pl.pallas_call(
        functools.partial(pick_kernel, wanted=tuple(wanted), groups=groups, size=size),
        out_shape=[jax.ShapeDtypeStruct((share, size, width), x.dtype)] * len(wanted),
        in_specs=[pl.BlockSpec(memory_space=pltpu.HBM)],
        out_specs=[vmem()] * len(wanted),
        scratch_shapes=[pltpu.SemaphoreType.DMA((len(wanted),))],
        compiler_params=params(CROWDED_BYTES),
        cost_estimate=pl.CostEstimate(
            flops=0,
            bytes_accessed=4 * share * size * width * len(wanted),
            transcendentals=0,
        ),
        name="picked",
    )(x)


FOLD = 8


def used_lanes(members):
    return members + 5


def low_lanes(members):
    rows = members // 2 - FOLD
    lane = lax.broadcasted_iota(jnp.int32, (rows, LANES), 1)
    row = lax.broadcasted_iota(jnp.int32, (rows, LANES), 0)
    first = used_lanes(members) - 2
    turn = used_lanes(members) - (LANES - used_lanes(members))
    folded = (row >= FOLD) & (row < 2 * FOLD) & (lane >= first + turn)
    return ((lane >= first) & (lane < first + 2)) | (folded & (lane < first + 2 + turn))


def gram_kernel(*refs, groups, share, blocks, width, unroll, first):
    parts = refs[:groups]
    scale_ref, weight_ref, own_ref, send_ref, rows_ref = refs[groups:]
    members = groups * share
    half = members // 2
    tiles = width // LANES
    pitch = rows_ref.shape[1] // members
    mem = lax.axis_index("mem")
    scale = scale_ref[first : first + blocks, :]
    for d in range(groups):
        base = (mem ^ d) * (share * pitch)

        def scale_member(k, carry, part=parts[d], base=base):
            value = (part[k].astype(F32) * scale).astype(BF16).astype(F32)
            start = base + k * pitch
            for t in range(tiles):
                rows_ref[t, pl.ds(start, blocks), :] = value[:, t * LANES : (t + 1) * LANES]
            return carry

        lax.fori_loop(0, share, scale_member, 0, unroll=4)

    used = used_lanes(members)
    spare = LANES - used
    packed_rows = half - FOLD
    lane = lax.broadcasted_iota(jnp.int32, (half, LANES), 1)
    row = lax.broadcasted_iota(jnp.int32, (half, LANES), 0)
    upper = (lane < half) & (lane > row)
    c_diagonal = lane == row + half
    from_bottom = (lane == members + 2) | (lane == members + 4)
    in_use = lax.broadcasted_iota(jnp.int32, (FOLD, LANES), 1) < used

    def block_group(i, carry):
        for u in range(unroll):
            b = i * unroll + u
            spread = jnp.concatenate(
                [rows_ref[t, pl.ds(b, members, stride=pitch), :] for t in range(tiles)], axis=1
            )
            weights = jnp.broadcast_to(weight_ref[pl.ds(first + b, 1), :], (8, width))
            filler = jnp.zeros((LANES - members - 8, width), F32)
            right = jnp.concatenate([spread, weights, filler], axis=0).astype(BF16)
            product = lax.dot_general(
                spread.astype(BF16), right, (((1,), (1,)), ((), ())), preferred_element_type=F32
            )
            top, bottom = product[:half], product[half:]
            diagonal = jnp.sum(jnp.where(c_diagonal, bottom, 0.0), axis=1, keepdims=True)
            packed = jnp.where(upper, pltpu.roll(bottom, LANES - half, axis=1), top)
            packed = jnp.where(from_bottom, bottom, packed)
            packed = jnp.where(lane == members, diagonal, packed)
            tail = packed[packed_rows:]
            own_ref[pl.ds(pl.multiple_of(b * packed_rows, 8), packed_rows), :] = jnp.concatenate(
                [
                    jnp.where(in_use, packed[:FOLD], pltpu.roll(tail, used, axis=1)),
                    jnp.where(
                        in_use, packed[FOLD : 2 * FOLD], pltpu.roll(tail, used - spare, axis=1)
                    ),
                    packed[2 * FOLD : packed_rows],
                ],
                axis=0,
            )
        return carry

    lax.fori_loop(0, blocks // unroll, block_group, 0)
    is_low = low_lanes(members)

    def finish(i, carry):
        at = pl.ds(pl.multiple_of(i * packed_rows, 16), packed_rows)
        value = own_ref[at, :]
        low = value - value.astype(BF16).astype(F32)
        send_ref[at, :] = jnp.where(is_low, low, value).astype(BF16)
        own_ref[at, :] = jnp.where(is_low, 0.0, value)
        return carry

    lax.fori_loop(0, blocks, finish, 0, unroll=4)


def packed_grams(parts, scale, weighted, first):
    groups = len(parts)
    share, blocks, width = parts[0].shape
    members = groups * share
    half = members // 2
    spare = LANES - used_lanes(members)
    assert half % 8 == 0 and (half - FOLD) % 16 == 0 and half >= 3 * FOLD
    assert spare >= used_lanes(members) - spare and members + 8 <= LANES
    flat = (blocks * (half - FOLD), LANES)
    return pl.pallas_call(
        functools.partial(
            gram_kernel,
            groups=groups,
            share=share,
            blocks=blocks,
            width=width,
            unroll=group_of(blocks),
            first=first,
        ),
        out_shape=(jax.ShapeDtypeStruct(flat, F32), jax.ShapeDtypeStruct(flat, BF16)),
        in_specs=[vmem()] * (groups + 2),
        out_specs=(vmem(), vmem()),
        scratch_shapes=[pltpu.VMEM((width // LANES, members * (blocks + PAD), LANES), F32)],
        compiler_params=params(),
        cost_estimate=pl.CostEstimate(
            flops=2 * blocks * members * width * LANES,
            bytes_accessed=members * blocks * width * 2,
            transcendentals=0,
        ),
        name="packed_grams",
    )(*parts, scale, weighted)


def blend_kernel(
    row_ref, taper_ref, *refs, members, neighbours, blocks, unroll, first
):
    *pieces, blend_ref, window_ref = refs
    half = members // 2
    used = used_lanes(members)
    spare = LANES - used
    packed_rows = half - FOLD
    filled = 0
    for piece in pieces:
        window_ref[pl.ds(filled, piece.shape[0]), :] = piece[...].astype(F32)
        filled += piece.shape[0]
    full = (members, LANES)
    lane = lax.broadcasted_iota(jnp.int32, full, 1)
    row = lax.broadcasted_iota(jnp.int32, full, 0)
    eye = (lane == row).astype(F32)
    in_matrix = lax.broadcasted_iota(jnp.int32, (1, LANES), 1) < members
    share_row = jnp.where(in_matrix, 1.0 / (members - 1), 0.0)
    half_lane = lax.broadcasted_iota(jnp.int32, (half, LANES), 1)
    half_row = lax.broadcasted_iota(jnp.int32, (half, LANES), 0)
    in_first = lax.broadcasted_iota(jnp.int32, (FOLD, LANES), 1) < spare
    pad_rows = jnp.zeros((LANES - half, LANES), F32)
    pad_depth = jnp.zeros((LANES - members, LANES), BF16)

    def total(x):
        return jnp.sum(jnp.sum(x, axis=0, keepdims=True), axis=1, keepdims=True)

    def times(lhs, rhs):
        return jnp.dot(
            lhs, jnp.concatenate([rhs, pad_depth], axis=0), preferred_element_type=F32
        )

    def localized_sum(b):
        packed = None
        for n in range(neighbours):
            start = pl.multiple_of(row_ref[first + b, n], 8)
            term = taper_ref[first + b, n] * window_ref[pl.ds(start, packed_rows), :]
            packed = term if packed is None else packed + term
        tail = jnp.where(
            in_first,
            pltpu.roll(packed[:FOLD], LANES - used, axis=1),
            pltpu.roll(packed[FOLD : 2 * FOLD], LANES - (used - spare), axis=1),
        )
        packed = jnp.concatenate([packed, tail], axis=0)
        turned = jnp.concatenate([packed, pad_rows], axis=0).T
        extra = turned[members : members + 8]
        lower = turned[:half]
        c_part = jnp.where(half_lane > half_row, packed, lower)
        c_part = jnp.where(half_lane == half_row, extra[0:1], c_part)
        top = jnp.where((half_lane > half_row) & (half_lane < half), lower, packed)
        bottom = jnp.where(half_lane < half, turned[half:members], pltpu.roll(c_part, half, axis=1))
        pull_row = (extra[1:2] + extra[3:4]) + pltpu.roll(extra[2:3] + extra[4:5], half, axis=1)
        return jnp.concatenate([top, bottom], axis=0) * share_row, pull_row

    def block_group(i, carry):
        group = range(unroll)
        ids = [i * unroll + u for u in group]
        sums = [localized_sum(b) for b in ids]
        gram = [g for g, _ in sums]
        trace = [total(g * eye) for g in gram]
        square = [total(g * g) for g in gram]
        frob2 = [square[u] + 2.0 * trace[u] + float(members) for u in group]
        inv = [lax.rsqrt(f) for f in frob2]
        mean = [t * (1.0 / members) for t in trace]
        y = [(1.0 + mean[u]) * inv[u] for u in group]
        y_rest = [(gram[u] - mean[u] * eye) * inv[u] for u in group]
        p = [-0.5 * v for v in y]
        p_rest = [-0.5 * v for v in y_rest]
        s = [1.5 + v for v in p]
        y_low = [v.astype(BF16) for v in y_rest]
        p_low = [v.astype(BF16) for v in p_rest]
        prod = [times(y_low[u], p_low[u]) for u in group]
        z = [-0.5 * v for v in s]
        z_rest = [-0.5 * v for v in p_rest]
        y_rest = [(s[u] * y_rest[u] + y[u] * p_rest[u]) + prod[u] for u in group]
        y = [s[u] * y[u] for u in group]
        for sweep in range(1, SWEEPS):
            last = sweep == SWEEPS - 1
            y_low = [v.astype(BF16) for v in y_rest]
            z_low = [v.astype(BF16) for v in z_rest]
            prod = [times(z_low[u], y_low[u]) for u in group]
            p = [z[u] * y[u] for u in group]
            p_rest = [(z[u] * y_rest[u] + y[u] * z_rest[u]) + prod[u] for u in group]
            s = [1.5 + v for v in p]
            p_low = [v.astype(BF16) for v in p_rest]
            if last:
                prod = [times(z_low[u], p_low[u]) for u in group]
                z_rest = [(s[u] * z_rest[u] + z[u] * p_rest[u]) + prod[u] for u in group]
            else:
                prod = [
                    times(jnp.concatenate([y_low[u], z_low[u]], axis=0), p_low[u])
                    for u in group
                ]
                y_rest = [
                    (s[u] * y_rest[u] + y[u] * p_rest[u]) + prod[u][:members] for u in group
                ]
                z_rest = [
                    (s[u] * z_rest[u] + z[u] * p_rest[u]) + prod[u][members:] for u in group
                ]
                y = [s[u] * y[u] for u in group]
            z = [s[u] * z[u] for u in group]
        root = [z[u] * eye + z_rest[u] for u in group]
        norm = [-2.0 * jnp.sqrt(v) for v in inv]
        inner = [
            jnp.sum(root[u] * sums[u][1], axis=1, keepdims=True) for u in group
        ]
        shift = [
            jnp.sum(root[u] * inner[u], axis=0, keepdims=True)
            * (norm[u] * norm[u] * (1.0 / (members - 1)))
            for u in group
        ]
        for u in group:
            at = pl.ds(pl.multiple_of(ids[u] * members, 16), members)
            blend_ref[at, :] = (norm[u] * root[u] + shift[u]).astype(BF16)
        return carry

    lax.fori_loop(0, blocks // unroll, block_group, 0)


def blends(rows, tapers, window, members, first, blocks):
    neighbours = rows.shape[1]
    window_rows = sum(piece.shape[0] for piece in window)
    return pl.pallas_call(
        functools.partial(
            blend_kernel,
            members=members,
            neighbours=neighbours,
            blocks=blocks,
            unroll=group_of(blocks),
            first=first,
        ),
        out_shape=jax.ShapeDtypeStruct((blocks * members, LANES), BF16),
        in_specs=[smem(), smem()] + [vmem()] * len(window),
        out_specs=vmem(),
        scratch_shapes=[pltpu.VMEM((window_rows, LANES), F32)],
        compiler_params=params(),
        cost_estimate=pl.CostEstimate(
            flops=blocks * 24 * members * members * LANES,
            bytes_accessed=3 * window_rows * LANES,
            transcendentals=0,
        ),
        name="blends",
    )(rows, tapers, *window)


def apply_kernel(*refs, groups, share, blocks, width, unroll):
    parts = refs[:groups]
    blend_ref = refs[groups]
    outs = refs[groups + 1 : 2 * groups + 1]
    center_ref, rows_ref = refs[2 * groups + 1 :]
    members = groups * share
    tiles = width // LANES
    pitch = rows_ref.shape[1] // members
    mem = lax.axis_index("mem")
    zero = jnp.zeros((blocks, width), F32)
    center = zero
    for d in range(groups):
        center = lax.fori_loop(
            0, share, lambda k, acc, part=parts[d]: acc + part[k].astype(F32), center, unroll=4
        )
    center = center * (1.0 / members)
    center_ref[...] = center
    for d in range(groups):
        base = (mem ^ d) * (share * pitch)

        def perturb(k, carry, part=parts[d], base=base):
            value = (part[k].astype(F32) - center_ref[...]).astype(BF16).astype(F32)
            start = base + k * pitch
            for t in range(tiles):
                rows_ref[t, pl.ds(start, blocks), :] = value[:, t * LANES : (t + 1) * LANES]
            return carry

        lax.fori_loop(0, share, perturb, 0, unroll=4)

    pad_depth = jnp.zeros((LANES - members, width), BF16)

    def block_group(i, carry):
        for u in range(unroll):
            b = i * unroll + u
            at = pl.ds(b, members, stride=pitch)
            anomalies = jnp.concatenate([rows_ref[t, at, :] for t in range(tiles)], axis=1)
            mixed = jnp.dot(
                blend_ref[pl.ds(pl.multiple_of(b * members, 16), members), :],
                jnp.concatenate([anomalies.astype(BF16), pad_depth], axis=0),
                preferred_element_type=F32,
            )
            for t in range(tiles):
                rows_ref[t, at, :] = mixed[:, t * LANES : (t + 1) * LANES]
        return carry

    lax.fori_loop(0, blocks // unroll, block_group, 0)

    for d in range(groups):
        base = (mem ^ d) * (share * pitch)

        def finish(k, carry, out=outs[d], base=base):
            start = base + k * pitch
            mixed = jnp.concatenate(
                [rows_ref[t, pl.ds(start, blocks), :] for t in range(tiles)], axis=1
            )
            out[k] = (center_ref[...] + mixed).astype(BF16)
            return carry

        lax.fori_loop(0, share, finish, 0, unroll=4)


def apply_blend(parts, blend):
    groups = len(parts)
    share, blocks, width = parts[0].shape
    members = groups * share
    part = jax.ShapeDtypeStruct((share, blocks, width), BF16)
    return pl.pallas_call(
        functools.partial(
            apply_kernel, groups=groups, share=share, blocks=blocks, width=width, unroll=group_of(blocks)
        ),
        out_shape=(part,) * groups,
        in_specs=[vmem()] * (groups + 1),
        out_specs=(vmem(),) * groups,
        scratch_shapes=[
            pltpu.VMEM((blocks, width), F32),
            pltpu.VMEM((width // LANES, members * (blocks + PAD), LANES), F32),
        ],
        compiler_params=params(),
        cost_estimate=pl.CostEstimate(
            flops=2 * blocks * members * LANES * width,
            bytes_accessed=2 * members * blocks * width * 2,
            transcendentals=0,
        ),
        name="apply_blend",
    )(*parts, blend)


def taper_of(offset):
    ratio = offset.astype(F32) / RADIUS
    return 1.0 / (1.0 + ratio * ratio)


def on_device(
    prior_fields,
    scaled_sensor_spread,
    measured_misfit,
    inverse_error_variance,
    active_sensor_number,
    adjacent_tiles,
):
    groups = lax.axis_size("mem")
    belts = lax.axis_size("lon")
    share, lon_rows, width = scaled_sensor_spread.shape
    members = groups * share
    half = members // 2
    total_blocks = lon_rows * belts
    blocks = lon_rows // groups
    assert groups & (groups - 1) == 0 and blocks == RADIUS
    mem = lax.axis_index("mem")
    lon = lax.axis_index("lon")
    flip = flip_of(groups)
    mine = mem ^ flip
    peers = [[(i, i ^ d) for i in range(groups)] for d in range(groups)]
    far_first = sorted(range(1, groups), key=lambda d: (d < groups // 2, d))

    def holder(g):
        belt, q = divmod(g % (belts * groups), groups)
        return (q ^ ((belt % 2) * (groups - 1))) * belts + belt

    ring = range(belts * groups)
    forward = [(holder(g), holder(g + 1)) for g in ring]
    backward = [(holder(g), holder(g - 1)) for g in ring]

    size = blocks // CHUNKS
    chunks = range(CHUNKS)
    last = None

    def pieces(x, wanted):
        nonlocal last
        taken = {}
        for d, c in wanted:
            if last is not None:
                x, _ = lax.optimization_barrier((x, last))
            start = ((mem ^ d) ^ flip) * blocks + c * size
            last = taken[d, c] = lax.dynamic_slice_in_dim(x, start, size, 1)
        return taken

    def own_rows(x):
        return lax.dynamic_slice_in_dim(x, mine * blocks, blocks, 0)

    def exchanged(taken, c):
        parts = {d: lax.ppermute(taken[d, c], "mem", peers[d]) for d in far_first}
        parts[0] = taken[0, c]
        return [parts[d] for d in range(groups)]

    order = far_first + [0]
    everything = [(d, c) for c in chunks for d in order]
    spread_taken = pieces(scaled_sensor_spread, everything[:1])
    gated, _ = lax.optimization_barrier((scaled_sensor_spread, last))
    (last,) = picked(gated, everything[1:2], groups, size)
    spread_taken |= {everything[1]: last} | pieces(scaled_sensor_spread, everything[2:])
    field_taken = pieces(prior_fields, everything)
    spread_parts = [exchanged(spread_taken, c) for c in chunks]
    field_parts = [exchanged(field_taken, c) for c in chunks]

    slot_ids = jnp.arange(width, dtype=jnp.int32)
    live = (slot_ids[None, :] < own_rows(active_sensor_number)[:, None]).astype(F32)
    obs_scale = jnp.sqrt(own_rows(inverse_error_variance) * live)
    weighted = own_rows(measured_misfit) * obs_scale
    local_ids = jnp.arange(blocks, dtype=jnp.int32)
    block_ids = lon * lon_rows + mine * blocks + local_ids
    offset_raw = jnp.mod(own_rows(adjacent_tiles) - block_ids[:, None], total_blocks)
    offset = jnp.where(offset_raw > total_blocks // 2, offset_raw - total_blocks, offset_raw)
    window_rows = (local_ids[:, None] % size + RADIUS + offset) * (half - FOLD)
    tapers = taper_of(offset)

    left, own, right = [], [], []
    for c in chunks:
        here, packed = packed_grams(
            spread_parts[c], obs_scale, weighted, c * size
        )
        own.append(here)
        left.append(lax.ppermute(packed, ("mem", "lon"), forward))
        right.append(lax.ppermute(packed, ("mem", "lon"), backward))
    window = left + own + right

    came = []
    for c in chunks:
        blend = blends(window_rows, tapers, window[c : c + 2 * CHUNKS + 1], members, c * size, size)
        out_parts = apply_blend(field_parts[c], blend)
        came.append((0, c, out_parts[0]))
        for d in far_first:
            came.append((d, c, lax.ppermute(out_parts[d], "mem", peers[d])))
    result = jnp.zeros(prior_fields.shape, BF16)
    for d, c, part in sorted(came, key=lambda item: (item[1], item[0] > 0, item[0] >= groups // 2)):
        start = ((mem ^ d) ^ flip) * blocks + c * size
        result = lax.dynamic_update_slice_in_dim(result, part, start, 1)
    return result


def solution(mesh):
    return jax.shard_map(
        on_device,
        mesh=mesh,
        in_specs=(
            P("mem", "lon", None),
            P("mem", "lon", None),
            P("lon", None),
            P("lon", None),
            P("lon"),
            P("lon", None),
        ),
        out_specs=P("mem", "lon", None),
        check_vma=False,
    )
```

```python
import functools

import jax
import jax.numpy as jnp
from jax import lax
from jax.experimental import pallas as pl
from jax.experimental.pallas import tpu as pltpu
from jax.sharding import PartitionSpec as P


RADIUS = 48
SWEEPS = 5
LANES = 128
F32 = jnp.float32
BF16 = jnp.bfloat16
VMEM_BYTES = 16 * 1024 * 1024
CROWDED_BYTES = 66_000_000
CHUNKS = 2
GROUP = 8
PAD = 1


def group_of(blocks):
    return max(u for u in range(1, GROUP + 1) if blocks % u == 0)


def vmem():
    return pl.BlockSpec(memory_space=pltpu.VMEM)


def smem():
    return pl.BlockSpec(memory_space=pltpu.SMEM)


def params(vmem_bytes=VMEM_BYTES):
    return pltpu.CompilerParams(vmem_limit_bytes=vmem_bytes)


def flip_of(groups):
    return (lax.axis_index("lon") % 2) * (groups - 1)


def pick_kernel(whole_ref, *refs, wanted, groups, size):
    outs, sems = refs[: len(wanted)], refs[len(wanted)]
    mem = lax.axis_index("mem")
    flip = flip_of(groups)
    copies = []
    for i, (d, c) in enumerate(wanted):
        start = ((mem ^ d) ^ flip) * (whole_ref.shape[1] // groups) + c * size
        rows = pl.ds(pl.multiple_of(start, 8), size)
        copies.append(pltpu.make_async_copy(whole_ref.at[:, rows, :], outs[i], sems.at[i]))
        copies[-1].start()
    for copy in copies:
        copy.wait()


def picked(x, wanted, groups, size):
    share, _, width = x.shape
    return pl.pallas_call(
        functools.partial(pick_kernel, wanted=tuple(wanted), groups=groups, size=size),
        out_shape=[jax.ShapeDtypeStruct((share, size, width), x.dtype)] * len(wanted),
        in_specs=[pl.BlockSpec(memory_space=pltpu.HBM)],
        out_specs=[vmem()] * len(wanted),
        scratch_shapes=[pltpu.SemaphoreType.DMA((len(wanted),))],
        compiler_params=params(CROWDED_BYTES),
        cost_estimate=pl.CostEstimate(
            flops=0,
            bytes_accessed=4 * share * size * width * len(wanted),
            transcendentals=0,
        ),
        name="picked",
    )(x)


FOLD = 8


def used_lanes(members):
    return members + 5


def low_lanes(members):
    rows = members // 2 - FOLD
    lane = lax.broadcasted_iota(jnp.int32, (rows, LANES), 1)
    row = lax.broadcasted_iota(jnp.int32, (rows, LANES), 0)
    first = used_lanes(members) - 2
    turn = used_lanes(members) - (LANES - used_lanes(members))
    folded = (row >= FOLD) & (row < 2 * FOLD) & (lane >= first + turn)
    return ((lane >= first) & (lane < first + 2)) | (folded & (lane < first + 2 + turn))


def gram_kernel(*refs, groups, share, blocks, width, unroll, first):
    parts = refs[:groups]
    scale_ref, weight_ref, own_ref, send_ref, rows_ref = refs[groups:]
    members = groups * share
    half = members // 2
    tiles = width // LANES
    pitch = rows_ref.shape[1] // members
    mem = lax.axis_index("mem")
    scale = scale_ref[first : first + blocks, :]
    for d in range(groups):
        base = (mem ^ d) * (share * pitch)

        def scale_member(k, carry, part=parts[d], base=base):
            value = (part[k].astype(F32) * scale).astype(BF16).astype(F32)
            start = base + k * pitch
            for t in range(tiles):
                rows_ref[t, pl.ds(start, blocks), :] = value[:, t * LANES : (t + 1) * LANES]
            return carry

        lax.fori_loop(0, share, scale_member, 0, unroll=4)

    used = used_lanes(members)
    spare = LANES - used
    packed_rows = half - FOLD
    lane = lax.broadcasted_iota(jnp.int32, (half, LANES), 1)
    row = lax.broadcasted_iota(jnp.int32, (half, LANES), 0)
    upper = (lane < half) & (lane > row)
    c_diagonal = lane == row + half
    from_bottom = (lane == members + 2) | (lane == members + 4)
    in_use = lax.broadcasted_iota(jnp.int32, (FOLD, LANES), 1) < used

    def block_group(i, carry):
        for u in range(unroll):
            b = i * unroll + u
            spread = jnp.concatenate(
                [rows_ref[t, pl.ds(b, members, stride=pitch), :] for t in range(tiles)], axis=1
            )
            weights = jnp.broadcast_to(weight_ref[pl.ds(first + b, 1), :], (8, width))
            filler = jnp.zeros((LANES - members - 8, width), F32)
            right = jnp.concatenate([spread, weights, filler], axis=0).astype(BF16)
            product = lax.dot_general(
                spread.astype(BF16), right, (((1,), (1,)), ((), ())), preferred_element_type=F32
            )
            top, bottom = product[:half], product[half:]
            diagonal = jnp.sum(jnp.where(c_diagonal, bottom, 0.0), axis=1, keepdims=True)
            packed = jnp.where(upper, pltpu.roll(bottom, LANES - half, axis=1), top)
            packed = jnp.where(from_bottom, bottom, packed)
            packed = jnp.where(lane == members, diagonal, packed)
            tail = packed[packed_rows:]
            own_ref[pl.ds(pl.multiple_of(b * packed_rows, 8), packed_rows), :] = jnp.concatenate(
                [
                    jnp.where(in_use, packed[:FOLD], pltpu.roll(tail, used, axis=1)),
                    jnp.where(
                        in_use, packed[FOLD : 2 * FOLD], pltpu.roll(tail, used - spare, axis=1)
                    ),
                    packed[2 * FOLD : packed_rows],
                ],
                axis=0,
            )
        return carry

    lax.fori_loop(0, blocks // unroll, block_group, 0)
    is_low = low_lanes(members)

    def finish(i, carry):
        at = pl.ds(pl.multiple_of(i * packed_rows, 16), packed_rows)
        value = own_ref[at, :]
        low = value - value.astype(BF16).astype(F32)
        send_ref[at, :] = jnp.where(is_low, low, value).astype(BF16)
        own_ref[at, :] = jnp.where(is_low, 0.0, value)
        return carry

    lax.fori_loop(0, blocks, finish, 0, unroll=4)


def packed_grams(parts, scale, weighted, first):
    groups = len(parts)
    share, blocks, width = parts[0].shape
    members = groups * share
    half = members // 2
    spare = LANES - used_lanes(members)
    assert half % 8 == 0 and (half - FOLD) % 16 == 0 and half >= 3 * FOLD
    assert spare >= used_lanes(members) - spare and members + 8 <= LANES
    flat = (blocks * (half - FOLD), LANES)
    return pl.pallas_call(
        functools.partial(
            gram_kernel,
            groups=groups,
            share=share,
            blocks=blocks,
            width=width,
            unroll=group_of(blocks),
            first=first,
        ),
        out_shape=(jax.ShapeDtypeStruct(flat, F32), jax.ShapeDtypeStruct(flat, BF16)),
        in_specs=[vmem()] * (groups + 2),
        out_specs=(vmem(), vmem()),
        scratch_shapes=[pltpu.VMEM((width // LANES, members * (blocks + PAD), LANES), F32)],
        compiler_params=params(),
        cost_estimate=pl.CostEstimate(
            flops=2 * blocks * members * width * LANES,
            bytes_accessed=members * blocks * width * 2,
            transcendentals=0,
        ),
        name="packed_grams",
    )(*parts, scale, weighted)


def blend_kernel(
    row_ref, taper_ref, *refs, members, neighbours, blocks, unroll, first
):
    *pieces, blend_ref, window_ref = refs
    half = members // 2
    used = used_lanes(members)
    spare = LANES - used
    packed_rows = half - FOLD
    filled = 0
    for piece in pieces:
        window_ref[pl.ds(filled, piece.shape[0]), :] = piece[...].astype(F32)
        filled += piece.shape[0]
    full = (members, LANES)
    lane = lax.broadcasted_iota(jnp.int32, full, 1)
    row = lax.broadcasted_iota(jnp.int32, full, 0)
    eye = (lane == row).astype(F32)
    in_matrix = lax.broadcasted_iota(jnp.int32, (1, LANES), 1) < members
    share_row = jnp.where(in_matrix, 1.0 / (members - 1), 0.0)
    half_lane = lax.broadcasted_iota(jnp.int32, (half, LANES), 1)
    half_row = lax.broadcasted_iota(jnp.int32, (half, LANES), 0)
    in_first = lax.broadcasted_iota(jnp.int32, (FOLD, LANES), 1) < spare
    pad_rows = jnp.zeros((LANES - half, LANES), F32)
    pad_depth = jnp.zeros((LANES - members, LANES), BF16)

    def total(x):
        return jnp.sum(jnp.sum(x, axis=0, keepdims=True), axis=1, keepdims=True)

    def times(lhs, rhs):
        return jnp.dot(
            lhs, jnp.concatenate([rhs, pad_depth], axis=0), preferred_element_type=F32
        )

    def localized_sum(b):
        packed = None
        for n in range(neighbours):
            start = pl.multiple_of(row_ref[first + b, n], 8)
            term = taper_ref[first + b, n] * window_ref[pl.ds(start, packed_rows), :]
            packed = term if packed is None else packed + term
        tail = jnp.where(
            in_first,
            pltpu.roll(packed[:FOLD], LANES - used, axis=1),
            pltpu.roll(packed[FOLD : 2 * FOLD], LANES - (used - spare), axis=1),
        )
        packed = jnp.concatenate([packed, tail], axis=0)
        turned = jnp.concatenate([packed, pad_rows], axis=0).T
        extra = turned[members : members + 8]
        lower = turned[:half]
        c_part = jnp.where(half_lane > half_row, packed, lower)
        c_part = jnp.where(half_lane == half_row, extra[0:1], c_part)
        top = jnp.where((half_lane > half_row) & (half_lane < half), lower, packed)
        bottom = jnp.where(half_lane < half, turned[half:members], pltpu.roll(c_part, half, axis=1))
        pull_row = (extra[1:2] + extra[3:4]) + pltpu.roll(extra[2:3] + extra[4:5], half, axis=1)
        return jnp.concatenate([top, bottom], axis=0) * share_row, pull_row

    def block_group(i, carry):
        group = range(unroll)
        ids = [i * unroll + u for u in group]
        sums = [localized_sum(b) for b in ids]
        gram = [g for g, _ in sums]
        trace = [total(g * eye) for g in gram]
        square = [total(g * g) for g in gram]
        frob2 = [square[u] + 2.0 * trace[u] + float(members) for u in group]
        inv = [lax.rsqrt(f) for f in frob2]
        mean = [t * (1.0 / members) for t in trace]
        y = [(1.0 + mean[u]) * inv[u] for u in group]
        y_rest = [(gram[u] - mean[u] * eye) * inv[u] for u in group]
        p = [-0.5 * v for v in y]
        p_rest = [-0.5 * v for v in y_rest]
        s = [1.5 + v for v in p]
        y_low = [v.astype(BF16) for v in y_rest]
        p_low = [v.astype(BF16) for v in p_rest]
        prod = [times(y_low[u], p_low[u]) for u in group]
        z = [-0.5 * v for v in s]
        z_rest = [-0.5 * v for v in p_rest]
        y_rest = [(s[u] * y_rest[u] + y[u] * p_rest[u]) + prod[u] for u in group]
        y = [s[u] * y[u] for u in group]
        for sweep in range(1, SWEEPS):
            last = sweep == SWEEPS - 1
            y_low = [v.astype(BF16) for v in y_rest]
            z_low = [v.astype(BF16) for v in z_rest]
            prod = [times(z_low[u], y_low[u]) for u in group]
            p = [z[u] * y[u] for u in group]
            p_rest = [(z[u] * y_rest[u] + y[u] * z_rest[u]) + prod[u] for u in group]
            s = [1.5 + v for v in p]
            p_low = [v.astype(BF16) for v in p_rest]
            if last:
                prod = [times(z_low[u], p_low[u]) for u in group]
                z_rest = [(s[u] * z_rest[u] + z[u] * p_rest[u]) + prod[u] for u in group]
            else:
                prod = [
                    times(jnp.concatenate([y_low[u], z_low[u]], axis=0), p_low[u])
                    for u in group
                ]
                y_rest = [
                    (s[u] * y_rest[u] + y[u] * p_rest[u]) + prod[u][:members] for u in group
                ]
                z_rest = [
                    (s[u] * z_rest[u] + z[u] * p_rest[u]) + prod[u][members:] for u in group
                ]
                y = [s[u] * y[u] for u in group]
            z = [s[u] * z[u] for u in group]
        root = [z[u] * eye + z_rest[u] for u in group]
        norm = [-2.0 * jnp.sqrt(v) for v in inv]
        inner = [
            jnp.sum(root[u] * sums[u][1], axis=1, keepdims=True) for u in group
        ]
        shift = [
            jnp.sum(root[u] * inner[u], axis=0, keepdims=True)
            * (norm[u] * norm[u] * (1.0 / (members - 1)))
            for u in group
        ]
        for u in group:
            at = pl.ds(pl.multiple_of(ids[u] * members, 16), members)
            blend_ref[at, :] = (norm[u] * root[u] + shift[u]).astype(BF16)
        return carry

    lax.fori_loop(0, blocks // unroll, block_group, 0)


def blends(rows, tapers, window, members, first, blocks):
    neighbours = rows.shape[1]
    window_rows = sum(piece.shape[0] for piece in window)
    return pl.pallas_call(
        functools.partial(
            blend_kernel,
            members=members,
            neighbours=neighbours,
            blocks=blocks,
            unroll=group_of(blocks),
            first=first,
        ),
        out_shape=jax.ShapeDtypeStruct((blocks * members, LANES), BF16),
        in_specs=[smem(), smem()] + [vmem()] * len(window),
        out_specs=vmem(),
        scratch_shapes=[pltpu.VMEM((window_rows, LANES), F32)],
        compiler_params=params(),
        cost_estimate=pl.CostEstimate(
            flops=blocks * 24 * members * members * LANES,
            bytes_accessed=3 * window_rows * LANES,
            transcendentals=0,
        ),
        name="blends",
    )(rows, tapers, *window)


def apply_kernel(*refs, groups, share, blocks, width, unroll):
    parts = refs[:groups]
    blend_ref = refs[groups]
    outs = refs[groups + 1 : 2 * groups + 1]
    center_ref, rows_ref = refs[2 * groups + 1 :]
    members = groups * share
    tiles = width // LANES
    pitch = rows_ref.shape[1] // members
    mem = lax.axis_index("mem")
    zero = jnp.zeros((blocks, width), F32)
    center = zero
    for d in range(groups):
        center = lax.fori_loop(
            0, share, lambda k, acc, part=parts[d]: acc + part[k].astype(F32), center, unroll=4
        )
    center = center * (1.0 / members)
    center_ref[...] = center
    for d in range(groups):
        base = (mem ^ d) * (share * pitch)

        def perturb(k, carry, part=parts[d], base=base):
            value = (part[k].astype(F32) - center_ref[...]).astype(BF16).astype(F32)
            start = base + k * pitch
            for t in range(tiles):
                rows_ref[t, pl.ds(start, blocks), :] = value[:, t * LANES : (t + 1) * LANES]
            return carry

        lax.fori_loop(0, share, perturb, 0, unroll=4)

    pad_depth = jnp.zeros((LANES - members, width), BF16)

    def block_group(i, carry):
        for u in range(unroll):
            b = i * unroll + u
            at = pl.ds(b, members, stride=pitch)
            anomalies = jnp.concatenate([rows_ref[t, at, :] for t in range(tiles)], axis=1)
            mixed = jnp.dot(
                blend_ref[pl.ds(pl.multiple_of(b * members, 16), members), :],
                jnp.concatenate([anomalies.astype(BF16), pad_depth], axis=0),
                preferred_element_type=F32,
            )
            for t in range(tiles):
                rows_ref[t, at, :] = mixed[:, t * LANES : (t + 1) * LANES]
        return carry

    lax.fori_loop(0, blocks // unroll, block_group, 0)

    for d in range(groups):
        base = (mem ^ d) * (share * pitch)

        def finish(k, carry, out=outs[d], base=base):
            start = base + k * pitch
            mixed = jnp.concatenate(
                [rows_ref[t, pl.ds(start, blocks), :] for t in range(tiles)], axis=1
            )
            out[k] = (center_ref[...] + mixed).astype(BF16)
            return carry

        lax.fori_loop(0, share, finish, 0, unroll=4)


def apply_blend(parts, blend):
    groups = len(parts)
    share, blocks, width = parts[0].shape
    members = groups * share
    part = jax.ShapeDtypeStruct((share, blocks, width), BF16)
    return pl.pallas_call(
        functools.partial(
            apply_kernel, groups=groups, share=share, blocks=blocks, width=width, unroll=group_of(blocks)
        ),
        out_shape=(part,) * groups,
        in_specs=[vmem()] * (groups + 1),
        out_specs=(vmem(),) * groups,
        scratch_shapes=[
            pltpu.VMEM((blocks, width), F32),
            pltpu.VMEM((width // LANES, members * (blocks + PAD), LANES), F32),
        ],
        compiler_params=params(),
        cost_estimate=pl.CostEstimate(
            flops=2 * blocks * members * LANES * width,
            bytes_accessed=2 * members * blocks * width * 2,
            transcendentals=0,
        ),
        name="apply_blend",
    )(*parts, blend)


def taper_of(offset):
    ratio = offset.astype(F32) / RADIUS
    return 1.0 / (1.0 + ratio * ratio)


def on_device(
    prior_fields,
    scaled_sensor_spread,
    measured_misfit,
    inverse_error_variance,
    active_sensor_number,
    adjacent_tiles,
):
    groups = lax.axis_size("mem")
    belts = lax.axis_size("lon")
    share, lon_rows, width = scaled_sensor_spread.shape
    members = groups * share
    half = members // 2
    total_blocks = lon_rows * belts
    blocks = lon_rows // groups
    assert groups & (groups - 1) == 0 and blocks == RADIUS
    mem = lax.axis_index("mem")
    lon = lax.axis_index("lon")
    flip = flip_of(groups)
    mine = mem ^ flip
    peers = [[(i, i ^ d) for i in range(groups)] for d in range(groups)]
    far_first = sorted(range(1, groups), key=lambda d: (d < groups // 2, d))

    def holder(g):
        belt, q = divmod(g % (belts * groups), groups)
        return (q ^ ((belt % 2) * (groups - 1))) * belts + belt

    ring = range(belts * groups)
    forward = [(holder(g), holder(g + 1)) for g in ring]
    backward = [(holder(g), holder(g - 1)) for g in ring]

    size = blocks // CHUNKS
    chunks = range(CHUNKS)
    last = None

    def after(x, earlier):
        return lax.optimization_barrier((x, earlier))[0]

    def sliced(x, wanted):
        nonlocal last
        taken = {}
        for d, c in wanted:
            if last is not None:
                x = after(x, last)
            start = ((mem ^ d) ^ flip) * blocks + c * size
            last = taken[d, c] = lax.dynamic_slice_in_dim(x, start, size, 1)
        return taken

    def own_rows(x):
        return lax.dynamic_slice_in_dim(x, mine * blocks, blocks, 0)

    def exchanged(taken, c):
        parts = {d: lax.ppermute(taken[d, c], "mem", peers[d]) for d in far_first}
        parts[0] = taken[0, c]
        return [parts[d] for d in range(groups)]

    order = far_first + [0]
    everything = [(d, c) for c in chunks for d in order]
    spread_taken = sliced(scaled_sensor_spread, everything[:1])
    (last,) = picked(after(scaled_sensor_spread, last), everything[1:2], groups, size)
    spread_taken |= {everything[1]: last} | sliced(scaled_sensor_spread, everything[2:])
    field_taken = sliced(prior_fields, everything[:2])
    spread_parts = [exchanged(spread_taken, c) for c in chunks]

    slot_ids = jnp.arange(width, dtype=jnp.int32)
    live = (slot_ids[None, :] < own_rows(active_sensor_number)[:, None]).astype(F32)
    obs_scale = jnp.sqrt(own_rows(inverse_error_variance) * live)
    weighted = own_rows(measured_misfit) * obs_scale
    local_ids = jnp.arange(blocks, dtype=jnp.int32)
    block_ids = lon * lon_rows + mine * blocks + local_ids
    offset_raw = jnp.mod(own_rows(adjacent_tiles) - block_ids[:, None], total_blocks)
    offset = jnp.where(offset_raw > total_blocks // 2, offset_raw - total_blocks, offset_raw)
    window_rows = (local_ids[:, None] % size + RADIUS + offset) * (half - FOLD)
    tapers = taper_of(offset)

    left, own, right = [], [], []
    for c in chunks:
        here, packed = packed_grams(
            spread_parts[c], obs_scale, weighted, c * size
        )
        own.append(here)
        left.append(lax.ppermute(packed, ("mem", "lon"), forward))
        right.append(lax.ppermute(packed, ("mem", "lon"), backward))
    last = own[-1]
    field_taken |= sliced(prior_fields, everything[2:])
    field_parts = [exchanged(field_taken, c) for c in chunks]
    window = left + own + right

    came = []
    for c in chunks:
        blend = blends(window_rows, tapers, window[c : c + 2 * CHUNKS + 1], members, c * size, size)
        out_parts = apply_blend(field_parts[c], blend)
        came.append((0, c, out_parts[0]))
        for d in far_first:
            came.append((d, c, lax.ppermute(out_parts[d], "mem", peers[d])))
    result = jnp.zeros(prior_fields.shape, BF16)
    for d, c, part in sorted(came, key=lambda item: (item[1], item[0] > 0, item[0] >= groups // 2)):
        start = ((mem ^ d) ^ flip) * blocks + c * size
        result = lax.dynamic_update_slice_in_dim(result, part, start, 1)
    return result


def solution(mesh):
    return jax.shard_map(
        on_device,
        mesh=mesh,
        in_specs=(
            P("mem", "lon", None),
            P("mem", "lon", None),
            P("lon", None),
            P("lon", None),
            P("lon"),
            P("lon", None),
        ),
        out_specs=P("mem", "lon", None),
        check_vma=False,
    )
```

```python
import functools

import jax
import jax.numpy as jnp
from jax import lax
from jax.experimental import pallas as pl
from jax.experimental.pallas import tpu as pltpu
from jax.sharding import PartitionSpec as P


RADIUS = 48
SWEEPS = 5
LANES = 128
F32 = jnp.float32
BF16 = jnp.bfloat16
VMEM_BYTES = 16 * 1024 * 1024
CROWDED_BYTES = 66_000_000
CHUNKS = 2
GROUP = 8
PAD = 1


def group_of(blocks):
    return max(u for u in range(1, GROUP + 1) if blocks % u == 0)


def vmem():
    return pl.BlockSpec(memory_space=pltpu.VMEM)


def smem():
    return pl.BlockSpec(memory_space=pltpu.SMEM)


def params(vmem_bytes=VMEM_BYTES):
    return pltpu.CompilerParams(vmem_limit_bytes=vmem_bytes)


def flip_of(groups):
    return (lax.axis_index("lon") % 2) * (groups - 1)


def pick_kernel(whole_ref, *refs, wanted, groups, size):
    outs, sems = refs[: len(wanted)], refs[len(wanted)]
    mem = lax.axis_index("mem")
    flip = flip_of(groups)
    copies = []
    for i, (d, c) in enumerate(wanted):
        start = ((mem ^ d) ^ flip) * (whole_ref.shape[1] // groups) + c * size
        rows = pl.ds(pl.multiple_of(start, 8), size)
        copies.append(pltpu.make_async_copy(whole_ref.at[:, rows, :], outs[i], sems.at[i]))
        copies[-1].start()
    for copy in copies:
        copy.wait()


def picked(x, wanted, groups, size):
    share, _, width = x.shape
    return pl.pallas_call(
        functools.partial(pick_kernel, wanted=tuple(wanted), groups=groups, size=size),
        out_shape=[jax.ShapeDtypeStruct((share, size, width), x.dtype)] * len(wanted),
        in_specs=[pl.BlockSpec(memory_space=pltpu.HBM)],
        out_specs=[vmem()] * len(wanted),
        scratch_shapes=[pltpu.SemaphoreType.DMA((len(wanted),))],
        compiler_params=params(CROWDED_BYTES),
        cost_estimate=pl.CostEstimate(
            flops=0,
            bytes_accessed=4 * share * size * width * len(wanted),
            transcendentals=0,
        ),
        name="picked",
    )(x)


FOLD = 8


def used_lanes(members):
    return members + 5


def low_lanes(members):
    rows = members // 2 - FOLD
    lane = lax.broadcasted_iota(jnp.int32, (rows, LANES), 1)
    row = lax.broadcasted_iota(jnp.int32, (rows, LANES), 0)
    first = used_lanes(members) - 2
    turn = used_lanes(members) - (LANES - used_lanes(members))
    folded = (row >= FOLD) & (row < 2 * FOLD) & (lane >= first + turn)
    return ((lane >= first) & (lane < first + 2)) | (folded & (lane < first + 2 + turn))


def gram_kernel(*refs, groups, share, blocks, width, unroll, first):
    parts = refs[:groups]
    scale_ref, weight_ref, own_ref, send_ref, rows_ref = refs[groups:]
    members = groups * share
    half = members // 2
    tiles = width // LANES
    pitch = rows_ref.shape[1] // members
    mem = lax.axis_index("mem")
    scale = scale_ref[first : first + blocks, :]
    for d in range(groups):
        base = (mem ^ d) * (share * pitch)

        def scale_member(k, carry, part=parts[d], base=base):
            value = (part[k].astype(F32) * scale).astype(BF16).astype(F32)
            start = base + k * pitch
            for t in range(tiles):
                rows_ref[t, pl.ds(start, blocks), :] = value[:, t * LANES : (t + 1) * LANES]
            return carry

        lax.fori_loop(0, share, scale_member, 0, unroll=4)

    used = used_lanes(members)
    spare = LANES - used
    packed_rows = half - FOLD
    lane = lax.broadcasted_iota(jnp.int32, (half, LANES), 1)
    row = lax.broadcasted_iota(jnp.int32, (half, LANES), 0)
    upper = (lane < half) & (lane > row)
    c_diagonal = lane == row + half
    from_bottom = (lane == members + 2) | (lane == members + 4)
    in_use = lax.broadcasted_iota(jnp.int32, (FOLD, LANES), 1) < used

    def block_group(i, carry):
        for u in range(unroll):
            b = i * unroll + u
            spread = jnp.concatenate(
                [rows_ref[t, pl.ds(b, members, stride=pitch), :] for t in range(tiles)], axis=1
            )
            weights = jnp.broadcast_to(weight_ref[pl.ds(first + b, 1), :], (8, width))
            filler = jnp.zeros((LANES - members - 8, width), F32)
            right = jnp.concatenate([spread, weights, filler], axis=0).astype(BF16)
            product = lax.dot_general(
                spread.astype(BF16), right, (((1,), (1,)), ((), ())), preferred_element_type=F32
            )
            top, bottom = product[:half], product[half:]
            diagonal = jnp.sum(jnp.where(c_diagonal, bottom, 0.0), axis=1, keepdims=True)
            packed = jnp.where(upper, pltpu.roll(bottom, LANES - half, axis=1), top)
            packed = jnp.where(from_bottom, bottom, packed)
            packed = jnp.where(lane == members, diagonal, packed)
            tail = packed[packed_rows:]
            own_ref[pl.ds(pl.multiple_of(b * packed_rows, 8), packed_rows), :] = jnp.concatenate(
                [
                    jnp.where(in_use, packed[:FOLD], pltpu.roll(tail, used, axis=1)),
                    jnp.where(
                        in_use, packed[FOLD : 2 * FOLD], pltpu.roll(tail, used - spare, axis=1)
                    ),
                    packed[2 * FOLD : packed_rows],
                ],
                axis=0,
            )
        return carry

    lax.fori_loop(0, blocks // unroll, block_group, 0)
    is_low = low_lanes(members)

    def finish(i, carry):
        at = pl.ds(pl.multiple_of(i * packed_rows, 16), packed_rows)
        value = own_ref[at, :]
        low = value - value.astype(BF16).astype(F32)
        send_ref[at, :] = jnp.where(is_low, low, value).astype(BF16)
        own_ref[at, :] = jnp.where(is_low, 0.0, value)
        return carry

    lax.fori_loop(0, blocks, finish, 0, unroll=4)


def packed_grams(parts, scale, weighted, first):
    groups = len(parts)
    share, blocks, width = parts[0].shape
    members = groups * share
    half = members // 2
    spare = LANES - used_lanes(members)
    assert half % 8 == 0 and (half - FOLD) % 16 == 0 and half >= 3 * FOLD
    assert spare >= used_lanes(members) - spare and members + 8 <= LANES
    flat = (blocks * (half - FOLD), LANES)
    return pl.pallas_call(
        functools.partial(
            gram_kernel,
            groups=groups,
            share=share,
            blocks=blocks,
            width=width,
            unroll=group_of(blocks),
            first=first,
        ),
        out_shape=(jax.ShapeDtypeStruct(flat, F32), jax.ShapeDtypeStruct(flat, BF16)),
        in_specs=[vmem()] * (groups + 2),
        out_specs=(vmem(), vmem()),
        scratch_shapes=[pltpu.VMEM((width // LANES, members * (blocks + PAD), LANES), F32)],
        compiler_params=params(),
        cost_estimate=pl.CostEstimate(
            flops=2 * blocks * members * width * LANES,
            bytes_accessed=members * blocks * width * 2,
            transcendentals=0,
        ),
        name="packed_grams",
    )(*parts, scale, weighted)


def blend_kernel(
    row_ref, taper_ref, *refs, members, neighbours, blocks, unroll, first
):
    *pieces, blend_ref, window_ref = refs
    half = members // 2
    used = used_lanes(members)
    spare = LANES - used
    packed_rows = half - FOLD
    filled = 0
    for piece in pieces:
        window_ref[pl.ds(filled, piece.shape[0]), :] = piece[...].astype(F32)
        filled += piece.shape[0]
    full = (members, LANES)
    lane = lax.broadcasted_iota(jnp.int32, full, 1)
    row = lax.broadcasted_iota(jnp.int32, full, 0)
    eye = (lane == row).astype(F32)
    in_matrix = lax.broadcasted_iota(jnp.int32, (1, LANES), 1) < members
    share_row = jnp.where(in_matrix, 1.0 / (members - 1), 0.0)
    half_lane = lax.broadcasted_iota(jnp.int32, (half, LANES), 1)
    half_row = lax.broadcasted_iota(jnp.int32, (half, LANES), 0)
    in_first = lax.broadcasted_iota(jnp.int32, (FOLD, LANES), 1) < spare
    pad_rows = jnp.zeros((LANES - half, LANES), F32)
    pad_depth = jnp.zeros((LANES - members, LANES), BF16)

    def total(x):
        return jnp.sum(jnp.sum(x, axis=0, keepdims=True), axis=1, keepdims=True)

    def times(lhs, rhs):
        return jnp.dot(
            lhs, jnp.concatenate([rhs, pad_depth], axis=0), preferred_element_type=F32
        )

    def localized_sum(b):
        packed = None
        for n in range(neighbours):
            start = pl.multiple_of(row_ref[first + b, n], 8)
            term = taper_ref[first + b, n] * window_ref[pl.ds(start, packed_rows), :]
            packed = term if packed is None else packed + term
        tail = jnp.where(
            in_first,
            pltpu.roll(packed[:FOLD], LANES - used, axis=1),
            pltpu.roll(packed[FOLD : 2 * FOLD], LANES - (used - spare), axis=1),
        )
        packed = jnp.concatenate([packed, tail], axis=0)
        turned = jnp.concatenate([packed, pad_rows], axis=0).T
        extra = turned[members : members + 8]
        lower = turned[:half]
        c_part = jnp.where(half_lane > half_row, packed, lower)
        c_part = jnp.where(half_lane == half_row, extra[0:1], c_part)
        top = jnp.where((half_lane > half_row) & (half_lane < half), lower, packed)
        bottom = jnp.where(half_lane < half, turned[half:members], pltpu.roll(c_part, half, axis=1))
        pull_row = (extra[1:2] + extra[3:4]) + pltpu.roll(extra[2:3] + extra[4:5], half, axis=1)
        return jnp.concatenate([top, bottom], axis=0) * share_row, pull_row

    def block_group(i, carry):
        group = range(unroll)
        ids = [i * unroll + u for u in group]
        sums = [localized_sum(b) for b in ids]
        gram = [g for g, _ in sums]
        trace = [total(g * eye) for g in gram]
        square = [total(g * g) for g in gram]
        frob2 = [square[u] + 2.0 * trace[u] + float(members) for u in group]
        inv = [lax.rsqrt(f) for f in frob2]
        mean = [t * (1.0 / members) for t in trace]
        y = [(1.0 + mean[u]) * inv[u] for u in group]
        y_rest = [(gram[u] - mean[u] * eye) * inv[u] for u in group]
        p = [-0.5 * v for v in y]
        p_rest = [-0.5 * v for v in y_rest]
        s = [1.5 + v for v in p]
        y_low = [v.astype(BF16) for v in y_rest]
        p_low = [v.astype(BF16) for v in p_rest]
        prod = [times(y_low[u], p_low[u]) for u in group]
        z = [-0.5 * v for v in s]
        z_rest = [-0.5 * v for v in p_rest]
        y_rest = [(s[u] * y_rest[u] + y[u] * p_rest[u]) + prod[u] for u in group]
        y = [s[u] * y[u] for u in group]
        for sweep in range(1, SWEEPS):
            last = sweep == SWEEPS - 1
            y_low = [v.astype(BF16) for v in y_rest]
            z_low = [v.astype(BF16) for v in z_rest]
            prod = [times(z_low[u], y_low[u]) for u in group]
            p = [z[u] * y[u] for u in group]
            p_rest = [(z[u] * y_rest[u] + y[u] * z_rest[u]) + prod[u] for u in group]
            s = [1.5 + v for v in p]
            p_low = [v.astype(BF16) for v in p_rest]
            if last:
                prod = [times(z_low[u], p_low[u]) for u in group]
                z_rest = [(s[u] * z_rest[u] + z[u] * p_rest[u]) + prod[u] for u in group]
            else:
                prod = [
                    times(jnp.concatenate([y_low[u], z_low[u]], axis=0), p_low[u])
                    for u in group
                ]
                y_rest = [
                    (s[u] * y_rest[u] + y[u] * p_rest[u]) + prod[u][:members] for u in group
                ]
                z_rest = [
                    (s[u] * z_rest[u] + z[u] * p_rest[u]) + prod[u][members:] for u in group
                ]
                y = [s[u] * y[u] for u in group]
            z = [s[u] * z[u] for u in group]
        root = [z[u] * eye + z_rest[u] for u in group]
        norm = [-2.0 * jnp.sqrt(v) for v in inv]
        inner = [
            jnp.sum(root[u] * sums[u][1], axis=1, keepdims=True) for u in group
        ]
        shift = [
            jnp.sum(root[u] * inner[u], axis=0, keepdims=True)
            * (norm[u] * norm[u] * (1.0 / (members - 1)))
            for u in group
        ]
        for u in group:
            at = pl.ds(pl.multiple_of(ids[u] * members, 16), members)
            blend_ref[at, :] = (norm[u] * root[u] + shift[u]).astype(BF16)
        return carry

    lax.fori_loop(0, blocks // unroll, block_group, 0)


def blends(rows, tapers, window, members, first, blocks):
    neighbours = rows.shape[1]
    window_rows = sum(piece.shape[0] for piece in window)
    return pl.pallas_call(
        functools.partial(
            blend_kernel,
            members=members,
            neighbours=neighbours,
            blocks=blocks,
            unroll=group_of(blocks),
            first=first,
        ),
        out_shape=jax.ShapeDtypeStruct((blocks * members, LANES), BF16),
        in_specs=[smem(), smem()] + [vmem()] * len(window),
        out_specs=vmem(),
        scratch_shapes=[pltpu.VMEM((window_rows, LANES), F32)],
        compiler_params=params(),
        cost_estimate=pl.CostEstimate(
            flops=blocks * 24 * members * members * LANES,
            bytes_accessed=3 * window_rows * LANES,
            transcendentals=0,
        ),
        name="blends",
    )(rows, tapers, *window)


def apply_kernel(*refs, groups, share, blocks, width, unroll):
    parts = refs[:groups]
    blend_ref = refs[groups]
    outs = refs[groups + 1 : 2 * groups + 1]
    center_ref, rows_ref = refs[2 * groups + 1 :]
    members = groups * share
    tiles = width // LANES
    pitch = rows_ref.shape[1] // members
    mem = lax.axis_index("mem")
    zero = jnp.zeros((blocks, width), F32)
    center = zero
    for d in range(groups):
        center = lax.fori_loop(
            0, share, lambda k, acc, part=parts[d]: acc + part[k].astype(F32), center, unroll=4
        )
    center = center * (1.0 / members)
    center_ref[...] = center
    for d in range(groups):
        base = (mem ^ d) * (share * pitch)

        def perturb(k, carry, part=parts[d], base=base):
            value = (part[k].astype(F32) - center_ref[...]).astype(BF16).astype(F32)
            start = base + k * pitch
            for t in range(tiles):
                rows_ref[t, pl.ds(start, blocks), :] = value[:, t * LANES : (t + 1) * LANES]
            return carry

        lax.fori_loop(0, share, perturb, 0, unroll=4)

    pad_depth = jnp.zeros((LANES - members, width), BF16)

    def block_group(i, carry):
        for u in range(unroll):
            b = i * unroll + u
            at = pl.ds(b, members, stride=pitch)
            anomalies = jnp.concatenate([rows_ref[t, at, :] for t in range(tiles)], axis=1)
            mixed = jnp.dot(
                blend_ref[pl.ds(pl.multiple_of(b * members, 16), members), :],
                jnp.concatenate([anomalies.astype(BF16), pad_depth], axis=0),
                preferred_element_type=F32,
            )
            for t in range(tiles):
                rows_ref[t, at, :] = mixed[:, t * LANES : (t + 1) * LANES]
        return carry

    lax.fori_loop(0, blocks // unroll, block_group, 0)

    for d in range(groups):
        base = (mem ^ d) * (share * pitch)

        def finish(k, carry, out=outs[d], base=base):
            start = base + k * pitch
            mixed = jnp.concatenate(
                [rows_ref[t, pl.ds(start, blocks), :] for t in range(tiles)], axis=1
            )
            out[k] = (center_ref[...] + mixed).astype(BF16)
            return carry

        lax.fori_loop(0, share, finish, 0, unroll=4)


def apply_blend(parts, blend):
    groups = len(parts)
    share, blocks, width = parts[0].shape
    members = groups * share
    part = jax.ShapeDtypeStruct((share, blocks, width), BF16)
    return pl.pallas_call(
        functools.partial(
            apply_kernel, groups=groups, share=share, blocks=blocks, width=width, unroll=group_of(blocks)
        ),
        out_shape=(part,) * groups,
        in_specs=[vmem()] * (groups + 1),
        out_specs=(vmem(),) * groups,
        scratch_shapes=[
            pltpu.VMEM((blocks, width), F32),
            pltpu.VMEM((width // LANES, members * (blocks + PAD), LANES), F32),
        ],
        compiler_params=params(),
        cost_estimate=pl.CostEstimate(
            flops=2 * blocks * members * LANES * width,
            bytes_accessed=2 * members * blocks * width * 2,
            transcendentals=0,
        ),
        name="apply_blend",
    )(*parts, blend)


def taper_of(offset):
    ratio = offset.astype(F32) / RADIUS
    return 1.0 / (1.0 + ratio * ratio)


def on_device(
    prior_fields,
    scaled_sensor_spread,
    measured_misfit,
    inverse_error_variance,
    active_sensor_number,
    adjacent_tiles,
):
    groups = lax.axis_size("mem")
    belts = lax.axis_size("lon")
    share, lon_rows, width = scaled_sensor_spread.shape
    members = groups * share
    half = members // 2
    total_blocks = lon_rows * belts
    blocks = lon_rows // groups
    assert groups & (groups - 1) == 0 and blocks == RADIUS
    mem = lax.axis_index("mem")
    lon = lax.axis_index("lon")
    flip = flip_of(groups)
    mine = mem ^ flip
    peers = [[(i, i ^ d) for i in range(groups)] for d in range(groups)]
    far_first = sorted(range(1, groups), key=lambda d: (d < groups // 2, d))

    def holder(g):
        belt, q = divmod(g % (belts * groups), groups)
        return (q ^ ((belt % 2) * (groups - 1))) * belts + belt

    ring = range(belts * groups)
    forward = [(holder(g), holder(g + 1)) for g in ring]
    backward = [(holder(g), holder(g - 1)) for g in ring]

    size = blocks // CHUNKS
    chunks = range(CHUNKS)
    last = None

    def after(x, earlier):
        return lax.optimization_barrier((x, earlier))[0]

    def sliced(x, wanted):
        nonlocal last
        taken = {}
        for d, c in wanted:
            if last is not None:
                x = after(x, last)
            start = ((mem ^ d) ^ flip) * blocks + c * size
            last = taken[d, c] = lax.dynamic_slice_in_dim(x, start, size, 1)
        return taken

    def own_rows(x):
        return lax.dynamic_slice_in_dim(x, mine * blocks, blocks, 0)

    def exchanged(taken, c):
        parts = {d: lax.ppermute(taken[d, c], "mem", peers[d]) for d in far_first}
        parts[0] = taken[0, c]
        return [parts[d] for d in range(groups)]

    order = far_first + [0]
    everything = [(d, c) for c in chunks for d in order]
    spread_taken = sliced(scaled_sensor_spread, everything[:1])
    (last,) = picked(after(scaled_sensor_spread, last), everything[1:2], groups, size)
    spread_taken |= {everything[1]: last} | sliced(scaled_sensor_spread, everything[2:])
    spread_parts = [exchanged(spread_taken, c) for c in chunks]

    slot_ids = jnp.arange(width, dtype=jnp.int32)
    live = (slot_ids[None, :] < own_rows(active_sensor_number)[:, None]).astype(F32)
    obs_scale = jnp.sqrt(own_rows(inverse_error_variance) * live)
    weighted = own_rows(measured_misfit) * obs_scale
    local_ids = jnp.arange(blocks, dtype=jnp.int32)
    block_ids = lon * lon_rows + mine * blocks + local_ids
    offset_raw = jnp.mod(own_rows(adjacent_tiles) - block_ids[:, None], total_blocks)
    offset = jnp.where(offset_raw > total_blocks // 2, offset_raw - total_blocks, offset_raw)
    window_rows = (local_ids[:, None] % size + RADIUS + offset) * (half - FOLD)
    tapers = taper_of(offset)

    left, own, right = [], [], []
    for c in chunks:
        here, packed = packed_grams(
            spread_parts[c], obs_scale, weighted, c * size
        )
        own.append(here)
        if c == 0:
            last = here
            field_taken = sliced(prior_fields, everything[:1])
        left.append(lax.ppermute(packed, ("mem", "lon"), forward))
        right.append(lax.ppermute(packed, ("mem", "lon"), backward))
    last = own[-1]
    field_taken |= sliced(prior_fields, everything[1:])
    field_parts = [exchanged(field_taken, c) for c in chunks]
    window = left + own + right

    came = []
    for c in chunks:
        blend = blends(window_rows, tapers, window[c : c + 2 * CHUNKS + 1], members, c * size, size)
        out_parts = apply_blend(field_parts[c], blend)
        came.append((0, c, out_parts[0]))
        for d in far_first:
            came.append((d, c, lax.ppermute(out_parts[d], "mem", peers[d])))
    result = jnp.zeros(prior_fields.shape, BF16)
    for d, c, part in sorted(came, key=lambda item: (item[1], item[0] > 0, item[0] >= groups // 2)):
        start = ((mem ^ d) ^ flip) * blocks + c * size
        result = lax.dynamic_update_slice_in_dim(result, part, start, 1)
    return result


def solution(mesh):
    return jax.shard_map(
        on_device,
        mesh=mesh,
        in_specs=(
            P("mem", "lon", None),
            P("mem", "lon", None),
            P("lon", None),
            P("lon", None),
            P("lon"),
            P("lon", None),
        ),
        out_specs=P("mem", "lon", None),
        check_vma=False,
    )
```
